32 devices in a mesh: dp: 16 (over z, x, core), fsdp: 2 (over y).
Axes of the slice: x: 2, y: 2, z: 4, core: 2. Of those that a mesh axis runs over, the one named last changes fastest.
Arguments:
- waveform: float32 [256, 400], P(('dp', 'fsdp')), may hold values from -6 to 6
- lengths: int32 [256], P(('dp', 'fsdp')), may hold values from 200 to 400, as said below
- owner_of: int32 [256], P(('dp', 'fsdp')), may hold values from 0 to 15, as said below
- targets: float32 [256, 39], P(('dp', 'fsdp')), may hold values from -5 to 5
- first_weight: float32 [10, 512], replicated, may hold values from -2 to 2
- first_gain: float32 [512], replicated, may hold values from 0.1 to 1.9
- first_shift: float32 [512], replicated, may hold values from -3 to 3
- second_weight: bfloat16 [1536, 512], P('fsdp'), may hold values from -0.15625 to 0.15625
- second_gain: float32 [512], replicated, may hold values from 0.1 to 1.9
- second_shift: float32 [512], replicated, may hold values from -3 to 3
Outputs:
- logvar: float32 [256, 39], P(('dp', 'fsdp'))
- loss: float32 [], replicated
- grad_second_weight: float32 [1536, 512], P('fsdp')
- grad_first_weight: float32 [10, 512], replicated
- grad_first_gain: float32 [512], replicated
- grad_first_shift: float32 [512], replicated
- grad_second_gain: float32 [512], replicated
- grad_second_shift: float32 [512], replicated
The draws below stay inside these ranges and needn't reach their ends.
Inputs may be any that keep to these rules, and one draw needn't show every extreme that they name: `lengths`: every draw has a row of length 400 and one of length 200. `owner_of`: rows read by the devices of one fsdp index go to owners of the same fsdp index. From one reader, each owner receives either no row or exactly 1 row; every owner receives exactly 8 rows.
All inputs are finite; a program needn't handle non-finite values.
Results may differ from the reference program's by a relative error of at most 0.0019.
Values may be sent and summed in bfloat16 or wider, within the bound.
No kernel may reach another device: no remote copies, remote signals or barrier semaphores. Data moves between devices by JAX's collectives and lax.ppermute only.
A program may use at most 64 MiB of HBM per device.

```python
import jax
import jax.numpy as jnp
from jax import lax

C = 512
LMAX = 400
RPD = 8
CAP = 1
F1 = 39
ROWS = 256
N_DP = 16
N_FSDP = 2


def draw_lengths(key, part):
    first_key, second_key, third_key = jax.random.split(key, 3)
    shortest = LMAX // 2
    lengths_drawn = jax.random.randint(first_key, (ROWS,), shortest, LMAX + 1)
    top_row = jax.random.randint(second_key, (), 0, ROWS)
    bottom_row = (top_row + 1 + jax.random.randint(third_key, (), 0, ROWS - 1)) % ROWS
    positions = jnp.arange(ROWS)
    lengths_drawn = jnp.where(positions == top_row, LMAX, lengths_drawn)
    lengths_drawn = jnp.where(positions == bottom_row, shortest, lengths_drawn)
    return lengths_drawn.astype(jnp.int32)


def shuffled_slots(sub_key):
    return jax.random.permutation(sub_key, RPD)


def one_column(column_key):
    base_key, shift_key, shuffle_key = jax.random.split(column_key, 3)
    groups = RPD // CAP
    readers = jax.random.permutation(base_key, N_DP)
    offsets = jax.random.permutation(shift_key, N_DP)[:groups]
    shuffles = jax.vmap(shuffled_slots)(jax.random.split(shuffle_key, N_DP))
    return (readers[:, None] + offsets[shuffles // CAP]) % N_DP


def draw_owner_of(key, part):
    column_keys = jax.random.split(jax.random.fold_in(key, 17), N_FSDP)
    owners = jax.vmap(one_column)(column_keys)
    return jnp.transpose(owners, (1, 0, 2)).reshape(ROWS).astype(jnp.int32)


def level_of(own_key, shape, shards, low, high):
    gain, own = 1.0, jax.random.fold_in(own_key, 6)
    for position, shards_of in shards:
        heights = jnp.exp(jax.random.uniform(jax.random.fold_in(own, position), (shards_of,), jnp.float32, low / len(shards), high / len(shards)))
        gain = gain * jnp.repeat(heights, shape[position] // shards_of).reshape([-1 if axis == position else 1 for axis in range(len(shape))])
    return gain


def centred(rng, shape, deviation, reach, cuts=(), kind=jnp.bfloat16):
    result = deviation * jax.random.normal(rng, shape, jnp.float32)
    if cuts:
        result = result * level_of(rng, shape, cuts, -0.22, 0.18)
    return jnp.clip(result, -reach, reach).astype(kind)


def setup_inputs(seed: int = 0) -> dict:
    seeds = jax.random.split(jax.random.key(seed), 11)
    waveform = centred(seeds[0], (ROWS, LMAX), 1.0, 6.0, ((0, 32),), jnp.float32)
    lengths = draw_lengths(jax.random.fold_in(seeds[10], 71), 0)
    owner_of = draw_owner_of(jax.random.fold_in(seeds[10], 71), 0)
    targets = centred(seeds[3], (ROWS, F1), 1.0, 5.0, ((0, 32),), jnp.float32)
    first_weight = centred(seeds[4], (10, C), 10 ** -0.5, 2.0, (), jnp.float32)
    first_gain = jnp.clip(1.0 + 0.18 * jax.random.normal(seeds[5], (C,), jnp.float32), 0.1, 1.9)
    first_shift = centred(seeds[6], (C,), 0.5, 3.0, (), jnp.float32)
    second_weight = centred(seeds[7], (3 * C, C), (3 * C) ** -0.5, 0.15625, ((0, 2),))
    second_gain = jnp.clip(1.0 + 0.18 * jax.random.normal(seeds[8], (C,), jnp.float32), 0.1, 1.9)
    second_shift = centred(seeds[9], (C,), 0.5, 3.0, (), jnp.float32)
    return dict(waveform=waveform, lengths=lengths, owner_of=owner_of, targets=targets, first_weight=first_weight, first_gain=first_gain, first_shift=first_shift, second_weight=second_weight, second_gain=second_gain, second_shift=second_shift)


epsilon = 1e-05

def layer_norm(values, norm_gain, norm_shift):
    row_mean = lax.optimization_barrier(jnp.mean(values, axis=-1, keepdims=True))
    centered = values - row_mean
    row_var = lax.optimization_barrier(jnp.mean(centered * centered, axis=-1, keepdims=True))
    return centered * lax.rsqrt(row_var + epsilon) * norm_gain + norm_shift

def first_layer(waveform, first_weight, first_gain, first_shift):
    row_total, samples = waveform.shape
    frames = samples // 5 - 1
    blocks = waveform.reshape(row_total, samples // 5, 5)
    windows = jnp.concatenate([blocks[:, :frames], blocks[:, 1:frames + 1]], axis=2)
    pre_norm = jnp.dot(windows.reshape(row_total * frames, 10), first_weight, precision=lax.Precision.HIGHEST, preferred_element_type=jnp.float32)
    return jax.nn.gelu(layer_norm(pre_norm, first_gain, first_shift), approximate=False)

def make_patches(activated, row_total):
    channels = activated.shape[1]
    frames = activated.shape[0] // row_total
    later = (frames - 1) // 2
    shaped = activated.reshape(row_total, frames, channels)
    padded = jnp.concatenate([shaped, jnp.zeros((row_total, 1, channels), activated.dtype)], axis=1)
    paired = padded.reshape(row_total, later + 1, 2, channels)
    even_frames = paired[:, :, 0]
    odd_frames = paired[:, :, 1]
    joined = jnp.concatenate([even_frames[:, :later], odd_frames[:, :later], even_frames[:, 1:]], axis=2)
    return joined.reshape(row_total * later, 3 * channels)

def patch_grad(grad_patches, row_total, frames):
    channels = grad_patches.shape[1] // 3
    later = grad_patches.shape[0] // row_total
    shaped = grad_patches.reshape(row_total, later, 3, channels)
    zero_frame = jnp.zeros((row_total, 1, channels), grad_patches.dtype)
    even_frames = jnp.concatenate([shaped[:, :, 0], zero_frame], axis=1) + jnp.concatenate([zero_frame, shaped[:, :, 2]], axis=1)
    odd_frames = jnp.concatenate([shaped[:, :, 1], zero_frame], axis=1)
    paired = jnp.stack([even_frames, odd_frames], axis=2).reshape(row_total, 2 * later + 2, channels)
    return paired[:, :frames].reshape(row_total * frames, channels)

def frame_mask_of(row_lengths, later):
    first_valid = (row_lengths - 10) // 5 + 1
    second_valid = (first_valid - 3) // 2 + 1
    inside = jnp.arange(later, dtype=jnp.int32)[None, :] < second_valid[:, None]
    return inside.astype(jnp.float32).reshape(-1)

def head_loss(second_pre, second_gain, second_shift, target_flat, frame_mask):
    activated = jax.nn.gelu(layer_norm(second_pre, second_gain, second_shift), approximate=False)
    row_mean = lax.optimization_barrier(jnp.mean(activated, axis=-1, keepdims=True))
    centered = activated - row_mean
    raw_logvar = jnp.log(lax.optimization_barrier(jnp.mean(centered * centered, axis=-1)) + epsilon)
    misfit = raw_logvar - target_flat
    return (jnp.sum(frame_mask * misfit * misfit), raw_logvar)

def reference(waveform, lengths, owner_of, targets, first_weight, first_gain, first_shift, second_weight, second_gain, second_shift):
    row_total = waveform.shape[0]
    positions = jnp.arange(row_total, dtype=jnp.int32)
    column = positions // RPD % N_FSDP
    sort_keys = (owner_of * N_FSDP + column) * row_total + positions
    row_order = jnp.argsort(sort_keys).astype(jnp.int32)
    owned_wave = jnp.take(waveform, row_order, axis=0)
    owned_length = jnp.take(lengths, row_order, axis=0)
    block_count = row_total // RPD
    later = LMAX // 10 - 1
    frames = LMAX // 5 - 1
    channels = first_weight.shape[1]
    wave_blocks = owned_wave.reshape(block_count, RPD, LMAX)
    length_blocks = owned_length.reshape(block_count, RPD)
    target_blocks = targets.reshape(block_count, RPD, later)

    def one_block(carried, block_item):
        wave_block, length_block, target_block = block_item

        def first_part(weight_first, gain_first, shift_first):
            return first_layer(wave_block, weight_first, gain_first, shift_first)
        activated, first_pull = jax.vjp(first_part, first_weight, first_gain, first_shift)
        rounded = activated.astype(jnp.bfloat16)
        patches = make_patches(rounded, RPD)
        second_pre = jnp.dot(patches, second_weight, preferred_element_type=jnp.float32)
        frame_mask = frame_mask_of(length_block, later)

        def head_part(pre_norm, gain_second, shift_second):
            return head_loss(pre_norm, gain_second, shift_second, target_block.reshape(-1), frame_mask)
        loss_sum, head_pull, raw_logvar = jax.vjp(head_part, second_pre, second_gain, second_shift, has_aux=True)
        grad_pre, grad_gain_two, grad_shift_two = head_pull(jnp.ones_like(loss_sum))
        grad_pre = grad_pre.astype(jnp.bfloat16)
        grad_weight_two = lax.dot_general(patches, grad_pre, (((0,), (0,)), ((), ())), preferred_element_type=jnp.float32)
        grad_patches = lax.dot_general(grad_pre, second_weight, (((1,), (1,)), ((), ())), preferred_element_type=jnp.float32)
        grad_act = patch_grad(grad_patches, RPD, frames)
        grad_weight_one, grad_gain_one, grad_shift_one = first_pull(grad_act)
        updated = (carried[0] + grad_weight_two, carried[1] + grad_weight_one, carried[2] + grad_gain_one, carried[3] + grad_shift_one, carried[4] + grad_gain_two, carried[5] + grad_shift_two, carried[6] + loss_sum, carried[7] + jnp.sum(frame_mask))
        return (updated, (raw_logvar * frame_mask).reshape(RPD, later))
    start_state = (jnp.zeros((3 * channels, channels), jnp.float32), jnp.zeros((10, channels), jnp.float32), jnp.zeros((channels,), jnp.float32), jnp.zeros((channels,), jnp.float32), jnp.zeros((channels,), jnp.float32), jnp.zeros((channels,), jnp.float32), jnp.zeros((), jnp.float32), jnp.zeros((), jnp.float32))
    final_state, logvar_blocks = lax.scan(one_block, start_state, (wave_blocks, length_blocks, target_blocks))
    logvar = logvar_blocks.reshape(row_total, later)
    loss = final_state[6] / final_state[7]
    return (logvar, loss, final_state[0], final_state[1], final_state[2], final_state[3], final_state[4], final_state[5])
```

```python
import jax
import jax.numpy as jnp
from jax import lax
from jax.sharding import PartitionSpec as P

epsilon = 1e-05
HIGHEST = lax.Precision.HIGHEST


def power_of_two(value):
    return value & (value - 1) == 0


def digits_of(size):
    digits = []
    stride, left = 1, size
    if left > 1:
        digits.append((stride, 2))
        stride, left = 2, left // 2
    while left > 1:
        radix = 2 if left in (2, 8, 32, 128) else 4
        digits.append((stride, radix))
        stride, left = stride * radix, left // radix
    return digits


def swap(values, axis_name, mask):
    size = lax.axis_size(axis_name)
    return lax.ppermute(values, axis_name, [(i, i ^ mask) for i in range(size)])


def gather_relative(values, axis_name):
    size = lax.axis_size(axis_name)
    step = 1
    while step < size:
        values = jnp.concatenate([values, swap(values, axis_name, step)], axis=0)
        step *= 2
    return values


def sum_everywhere(values, axis_sizes):
    for axis_name, size in axis_sizes:
        step = 1
        while step < size:
            values = values + swap(values, axis_name, step)
            step *= 2
    return values


def part_of(values, index, count):
    size = values.shape[0] // count
    return lax.dynamic_slice_in_dim(values, index * size, size, axis=0)


def scatter_sum(values, axis_name, stride, radix, link_type):
    digit = lax.axis_index(axis_name) // stride % radix
    total = part_of(values, digit, radix).astype(jnp.float32)
    for other in range(1, radix):
        sent = part_of(values, digit ^ other, radix).astype(link_type)
        total = total + swap(sent, axis_name, other * stride).astype(jnp.float32)
    return total


def gather_parts(values, axis_name, stride, radix):
    digit = lax.axis_index(axis_name) // stride % radix
    parts = [values] + [swap(values, axis_name, other * stride) for other in range(1, radix)]
    size = values.shape[0]
    whole = jnp.zeros((radix * size,) + values.shape[1:], values.dtype)
    for other in range(radix):
        whole = lax.dynamic_update_slice_in_dim(whole, parts[other], (digit ^ other) * size, axis=0)
    return whole


def gather_weight(weight, cores):
    if lax.axis_size("fsdp") != 2 or not cores:
        return lax.all_gather(weight, "fsdp", axis=0, tiled=True)
    core = lax.axis_index("dp") % 2
    fetched = swap(part_of(weight, core, 2), "fsdp", 1)
    others = swap(fetched, "dp", 1)
    missing = jnp.where(
        core == 0,
        jnp.concatenate([fetched, others], axis=0),
        jnp.concatenate([others, fetched], axis=0),
    )
    return jnp.where(
        lax.axis_index("fsdp") == 0,
        jnp.concatenate([weight, missing], axis=0),
        jnp.concatenate([missing, weight], axis=0),
    )


def normalized(values):
    row_mean = jnp.mean(values, axis=-1, keepdims=True)
    centered = values - row_mean
    row_var = jnp.mean(centered * centered, axis=-1, keepdims=True)
    scale = lax.rsqrt(row_var + epsilon)
    return centered * scale, scale


def gelu_parts(values):
    share = 0.5 * lax.erfc(values * (-(0.5**0.5)))
    density = jnp.exp(-0.5 * values * values) * 0.3989422804014327
    return values * share, share + values * density


def norm_pull(grad_out, unit, scale, gain):
    grad_unit = grad_out * gain
    first = jnp.mean(grad_unit, axis=-1, keepdims=True)
    second = jnp.mean(grad_unit * unit, axis=-1, keepdims=True)
    grad_raw = scale * (grad_unit - first - unit * second)
    return grad_raw, jnp.sum(grad_out * unit, axis=0), jnp.sum(grad_out, axis=0)


def per_device(
    waveform,
    lengths,
    owner_of,
    targets,
    first_weight,
    first_gain,
    first_shift,
    second_weight,
    second_gain,
    second_shift,
):
    peers, groups = lax.axis_size("dp"), lax.axis_size("fsdp")
    rows, samples = waveform.shape
    later = targets.shape[1]
    frames = samples // 5 - 1
    channels = first_weight.shape[1]
    doubling = power_of_two(peers) and power_of_two(groups)
    me = lax.axis_index("dp")

    weight = gather_weight(second_weight, doubling and peers > 1)

    noted = jnp.concatenate([targets, owner_of.astype(jnp.float32)[:, None]], axis=1)
    if doubling:
        known = gather_relative(noted, "dp")
        reader = me ^ (jnp.arange(peers * rows, dtype=jnp.int32) // rows)
    else:
        known = lax.all_gather(noted, "dp", axis=0, tiled=True)
        reader = jnp.arange(peers * rows, dtype=jnp.int32) // rows
    known_owner = known[:, later].astype(jnp.int32)
    known_targets = known[:, :later]
    same_owner = owner_of[:, None] == known_owner[None, :]
    slot = jnp.sum((same_owner & (reader < me)[None, :]).astype(jnp.int32), axis=1)
    held = jnp.arange(peers * rows, dtype=jnp.int32) % rows
    wanted = (reader[None, :] == owner_of[:, None]) & (held[None, :] == slot[:, None])
    row_targets = lax.dot_general(
        known_targets,
        wanted.astype(jnp.float32),
        (((0,), (1,)), ((), ())),
        precision=HIGHEST,
        preferred_element_type=jnp.float32,
    ).reshape(later * rows, 1)
    mine = known_owner == me
    arrival = jnp.sum((mine[None, :] & (reader[None, :] < reader[:, None])).astype(jnp.int32), axis=1)
    picking = (
        mine[None, :] & (arrival[None, :] == jnp.arange(rows, dtype=jnp.int32)[:, None])
    ).astype(jnp.float32)

    blocks = waveform.reshape(rows, samples // 5, 5).transpose(1, 0, 2)
    windows = jnp.concatenate([blocks[:frames], blocks[1 : frames + 1]], axis=2)
    windows = windows.reshape(frames * rows, 10)
    first_pre = jnp.dot(
        windows, first_weight, precision=HIGHEST, preferred_element_type=jnp.float32
    )
    first_unit, first_scale = normalized(first_pre)
    activated, first_slope = gelu_parts(first_unit * first_gain + first_shift)
    rounded = activated.astype(jnp.bfloat16).reshape(frames, rows, channels)
    even, odd = rounded[0::2], rounded[1::2]
    patches = jnp.concatenate([even[:later], odd, even[1:]], axis=2)
    patches = patches.reshape(later * rows, 3 * channels)

    second_pre = jnp.dot(patches, weight, preferred_element_type=jnp.float32)
    second_unit, second_scale = normalized(second_pre)
    second_act, second_slope = gelu_parts(second_unit * second_gain + second_shift)
    act_mean = jnp.mean(second_act, axis=-1, keepdims=True)
    act_centered = second_act - act_mean
    act_var = jnp.mean(act_centered * act_centered, axis=-1, keepdims=True) + epsilon
    raw_logvar = jnp.log(act_var)
    first_valid = (lengths - 10) // 5 + 1
    second_valid = (first_valid - 3) // 2 + 1
    frame_mask = (
        jnp.arange(later, dtype=jnp.int32)[:, None] < second_valid[None, :]
    ).astype(jnp.float32)
    frame_mask = frame_mask.reshape(later * rows, 1)
    misfit = raw_logvar - row_targets
    loss_sum = jnp.sum(frame_mask * misfit * misfit)
    frame_count = jnp.sum(frame_mask)
    pull = frame_mask * misfit / act_var * (4.0 / channels)
    grad_pre, grad_gain_two, grad_shift_two = norm_pull(
        pull * act_centered * second_slope, second_unit, second_scale, second_gain
    )
    grad_pre = grad_pre.astype(jnp.bfloat16)

    def weight_gradient(columns):
        return lax.dot_general(
            patches, columns, (((0,), (0,)), ((), ())), preferred_element_type=jnp.float32
        )

    if doubling and peers > 1:
        half = channels // 2
        core = me % 2
        sent = weight_gradient(lax.dynamic_slice_in_dim(grad_pre, (1 - core) * half, half, 1))
        kept = weight_gradient(lax.dynamic_slice_in_dim(grad_pre, core * half, half, 1))
        total = kept + swap(sent, "dp", 1)
        stride = groups
        while stride > 1:
            stride //= 2
            total = scatter_sum(total, "fsdp", stride, 2, jnp.bfloat16)
        digits = digits_of(peers)[1:]
        for position, (stride, radix) in enumerate(digits):
            kind = jnp.bfloat16 if position == 0 and len(digits) > 1 else jnp.float32
            total = scatter_sum(total, "dp", stride, radix, kind)
        for stride, radix in digits[::-1]:
            total = gather_parts(total, "dp", stride, radix)
        other_half = swap(total, "dp", 1)
        grad_weight_two = jnp.where(
            core == 0,
            jnp.concatenate([total, other_half], axis=1),
            jnp.concatenate([other_half, total], axis=1),
        )
    else:
        grad_weight_two = lax.psum(
            lax.psum_scatter(
                weight_gradient(grad_pre), "fsdp", scatter_dimension=0, tiled=True
            ),
            "dp",
        )

    grad_patches = lax.dot_general(
        grad_pre, weight, (((1,), (1,)), ((), ())), preferred_element_type=jnp.float32
    ).reshape(later, rows, 3 * channels)
    zero_frame = jnp.zeros((1, rows, channels), jnp.float32)
    grad_even = jnp.concatenate([grad_patches[:, :, :channels], zero_frame], axis=0)
    grad_even = grad_even + jnp.concatenate([zero_frame, grad_patches[:, :, 2 * channels :]], axis=0)
    grad_odd = jnp.concatenate([grad_patches[:, :, channels : 2 * channels], zero_frame], axis=0)
    grad_act = jnp.stack([grad_even, grad_odd], axis=1).reshape(2 * later + 2, rows, channels)
    grad_act = grad_act[:frames].reshape(frames * rows, channels)
    grad_first, grad_gain_one, grad_shift_one = norm_pull(
        grad_act * first_slope, first_unit, first_scale, first_gain
    )
    grad_weight_one = lax.dot_general(
        windows,
        grad_first,
        (((0,), (0,)), ((), ())),
        precision=HIGHEST,
        preferred_element_type=jnp.float32,
    )
    scalars = jnp.concatenate(
        [loss_sum.reshape(1), frame_count.reshape(1), jnp.zeros((channels - 2,), jnp.float32)]
    )
    small = jnp.concatenate(
        [
            grad_weight_one,
            jnp.stack([grad_gain_one, grad_shift_one, grad_gain_two, grad_shift_two, scalars]),
            jnp.zeros((1, channels), jnp.float32),
        ],
        axis=0,
    )
    own_logvar = (raw_logvar * frame_mask).reshape(later, rows).T
    if doubling:
        small = sum_everywhere(small, (("dp", peers), ("fsdp", groups)))
        all_logvar = gather_relative(own_logvar, "dp")
    else:
        small = lax.psum(small, ("dp", "fsdp"))
        all_logvar = lax.all_gather(own_logvar, "dp", axis=0, tiled=True)
    logvar = jnp.dot(
        picking, all_logvar, precision=HIGHEST, preferred_element_type=jnp.float32
    )
    loss = small[14, 0] / small[14, 1]
    return (logvar, loss, grad_weight_two, small[:10], small[10], small[11], small[12], small[13])


def solution(mesh):
    placed = (
        P(("dp", "fsdp"), None),
        P(("dp", "fsdp")),
        P(("dp", "fsdp")),
        P(("dp", "fsdp"), None),
        P(),
        P(),
        P(),
        P("fsdp", None),
        P(),
        P(),
    )
    return jax.shard_map(
        per_device,
        mesh=mesh,
        in_specs=placed,
        out_specs=(P(("dp", "fsdp"), None), P(), P("fsdp", None), P(), P(), P(), P(), P()),
        check_vma=False,
    )
```

```python
import jax
import jax.numpy as jnp
from jax import lax
from jax.sharding import PartitionSpec as P

epsilon = 1e-05
HIGHEST = lax.Precision.HIGHEST


def tie(*values):
    return lax.optimization_barrier(values)


def power_of_two(value):
    return value & (value - 1) == 0


def swap(values, axis_name, mask):
    size = lax.axis_size(axis_name)
    return lax.ppermute(values, axis_name, [(i, i ^ mask) for i in range(size)])


def part_of(values, index, count):
    size = values.shape[0] // count
    return lax.dynamic_slice_in_dim(values, index * size, size, axis=0)


def packed(values, exponent):
    (scale,) = tie(jnp.exp2(14.0 - exponent))
    note = jnp.broadcast_to(exponent, (8, values.shape[1]))
    return jnp.concatenate([values * scale, note], axis=0).astype(jnp.float16)


def added(total, exponent, message):
    received = message[-8:].astype(jnp.float32)[:1]
    scale, larger = tie(jnp.exp2(received - 14.0), jnp.maximum(received, exponent) + 1.0)
    return total + message[:-8].astype(jnp.float32) * scale, larger


def scatter_message(total, exponent, axis_name, mask):
    bit = jnp.minimum(lax.axis_index(axis_name) & mask, 1)
    return packed(part_of(total, 1 - bit, 2), exponent)


def scatter_sum(total, exponent, message, axis_name, mask):
    bit = jnp.minimum(lax.axis_index(axis_name) & mask, 1)
    return added(part_of(total, bit, 2), exponent, swap(message, axis_name, mask))


def gather_pair(values, axis_name, mask):
    bit = jnp.minimum(lax.axis_index(axis_name) & mask, 1)
    size = values.shape[0]
    whole = jnp.zeros((2 * size,) + values.shape[1:], values.dtype)
    whole = lax.dynamic_update_slice_in_dim(whole, values, bit * size, axis=0)
    other = swap(values, axis_name, mask)
    return lax.dynamic_update_slice_in_dim(whole, other, (1 - bit) * size, axis=0)


def normalized(values):
    row_mean = jnp.mean(values, axis=-1, keepdims=True)
    centered = values - row_mean
    row_var = jnp.mean(centered * centered, axis=-1, keepdims=True)
    scale = lax.rsqrt(row_var + epsilon)
    return centered * scale, scale


def gelu_share(values):
    return 0.5 * lax.erf(values * 0.5**0.5) + 0.5


def gelu_slope(values):
    return gelu_share(values) + values * jnp.exp(-0.5 * values * values) * 0.3989422804014327


def norm_pull(grad_out, unit, scale, gain):
    grad_unit = grad_out * gain
    first = jnp.mean(grad_unit, axis=-1, keepdims=True)
    second = jnp.mean(grad_unit * unit, axis=-1, keepdims=True)
    grad_raw = scale * (grad_unit - first - unit * second)
    return grad_raw, jnp.sum(grad_out * unit, axis=0), jnp.sum(grad_out, axis=0)


def per_device(
    waveform,
    lengths,
    owner_of,
    targets,
    first_weight,
    first_gain,
    first_shift,
    second_weight,
    second_gain,
    second_shift,
):
    peers, groups = lax.axis_size("dp"), lax.axis_size("fsdp")
    rows, samples = waveform.shape
    later = targets.shape[1]
    frames = samples // 5 - 1
    channels = first_weight.shape[1]
    staged = power_of_two(peers) and power_of_two(groups) and peers >= 4 and groups > 1
    core, side = lax.axis_index("dp") % 2, lax.axis_index("dp") // 2 % 2

    fetched = None
    if staged and groups == 2:
        fetched = swap(part_of(second_weight, core, 2), "fsdp", 1)

    width = samples + 1
    noted = jnp.concatenate([waveform, lengths.astype(jnp.float32)[:, None]], axis=1)
    per_owner = max(1, 2 * rows // peers)
    matches = (owner_of[:, None] == owner_of[None, :]).astype(jnp.int32)
    slots = owner_of * per_owner + jnp.sum(jnp.tril(matches, -1), axis=1)
    placing = slots[:, None] == jnp.arange(peers * per_owner, dtype=jnp.int32)[None, :]
    sent = lax.dot_general(
        placing.astype(jnp.float32),
        noted,
        (((0,), (0,)), ((), ())),
        precision=HIGHEST,
        preferred_element_type=jnp.float32,
    )
    got = lax.all_to_all(sent, "dp", split_axis=0, concat_axis=0, tiled=True)
    present = got[:, samples] > 0.5
    arrival = jnp.cumsum(present.astype(jnp.int32)) - 1
    picking = present[None, :] & (
        arrival[None, :] == jnp.arange(rows, dtype=jnp.int32)[:, None]
    )
    owned = jnp.dot(
        picking.astype(jnp.float32), got, precision=HIGHEST, preferred_element_type=jnp.float32
    )
    waveform, lengths = owned[:, :samples], owned[:, samples].astype(jnp.int32)

    blocks = waveform.reshape(rows, samples // 5, 5).transpose(1, 0, 2)
    windows = jnp.concatenate([blocks[:frames], blocks[1 : frames + 1]], axis=2)
    windows = windows.reshape(frames * rows, 10)
    if fetched is None:
        weight = lax.all_gather(second_weight, "fsdp", axis=0, tiled=True)
    else:
        windows, fetched = tie(windows, fetched)
        fetched_others = swap(fetched, "dp", 1)
        missing = jnp.where(
            core == 0,
            jnp.concatenate([fetched, fetched_others], axis=0),
            jnp.concatenate([fetched_others, fetched], axis=0),
        )
        weight = jnp.where(
            lax.axis_index("fsdp") == 0,
            jnp.concatenate([second_weight, missing], axis=0),
            jnp.concatenate([missing, second_weight], axis=0),
        )
    first_pre = jnp.dot(
        windows, first_weight, precision=HIGHEST, preferred_element_type=jnp.float32
    )
    first_unit, first_scale = normalized(first_pre)
    first_normed = first_unit * first_gain + first_shift
    activated = first_normed * gelu_share(first_normed)
    rounded = activated.astype(jnp.bfloat16).reshape(frames, rows, channels)
    even, odd = rounded[0::2], rounded[1::2]
    patches = jnp.concatenate([even[:later], odd, even[1:]], axis=2)
    patches = patches.reshape(later * rows, 3 * channels)

    second_pre = jnp.dot(patches, weight, preferred_element_type=jnp.float32)
    second_unit, second_scale = normalized(second_pre)
    second_normed = second_unit * second_gain + second_shift
    second_share = gelu_share(second_normed)
    second_act = second_normed * second_share
    second_slope = second_share + second_normed * (
        jnp.exp(-0.5 * second_normed * second_normed) * 0.3989422804014327
    )
    act_mean = jnp.mean(second_act, axis=-1, keepdims=True)
    act_centered = second_act - act_mean
    act_var = jnp.mean(act_centered * act_centered, axis=-1, keepdims=True) + epsilon
    raw_logvar = jnp.log(act_var)
    first_valid = (lengths - 10) // 5 + 1
    second_valid = (first_valid - 3) // 2 + 1
    frame_mask = (
        jnp.arange(later, dtype=jnp.int32)[:, None] < second_valid[None, :]
    ).astype(jnp.float32)
    frame_mask = frame_mask.reshape(later * rows, 1)
    misfit = raw_logvar - targets.T.reshape(later * rows, 1)
    pull = frame_mask * misfit / act_var * (4.0 / channels)
    grad_pre, grad_gain_two, grad_shift_two = norm_pull(
        pull * act_centered * second_slope, second_unit, second_scale, second_gain
    )
    grad_pre = grad_pre.astype(jnp.bfloat16)

    def product(columns):
        return lax.dot_general(
            columns, grad_pre, (((0,), (0,)), ((), ())), preferred_element_type=jnp.float32
        )

    def backward(grad_pre, misfit, windows, first_unit, grad_gain_two, grad_shift_two):
        first_normed = first_unit * first_gain + first_shift
        grad_patches = lax.dot_general(
            grad_pre, weight, (((1,), (1,)), ((), ())), preferred_element_type=jnp.float32
        ).reshape(later, rows, 3 * channels)
        zero_frame = jnp.zeros((1, rows, channels), jnp.float32)
        grad_even = jnp.concatenate([grad_patches[:, :, :channels], zero_frame], axis=0)
        grad_even = grad_even + jnp.concatenate(
            [zero_frame, grad_patches[:, :, 2 * channels :]], axis=0
        )
        grad_odd = jnp.concatenate([grad_patches[:, :, channels : 2 * channels], zero_frame], axis=0)
        grad_act = jnp.stack([grad_even, grad_odd], axis=1).reshape(2 * later + 2, rows, channels)
        grad_act = grad_act[:frames].reshape(frames * rows, channels)
        grad_first, grad_gain_one, grad_shift_one = norm_pull(
            grad_act * gelu_slope(first_normed), first_unit, first_scale, first_gain
        )
        grad_weight_one = lax.dot_general(
            windows,
            grad_first,
            (((0,), (0,)), ((), ())),
            precision=HIGHEST,
            preferred_element_type=jnp.float32,
        )
        loss_sum = jnp.sum(frame_mask * misfit * misfit, axis=0, keepdims=True)
        frame_count = jnp.sum(frame_mask, axis=0, keepdims=True)
        return jnp.concatenate(
            [
                grad_weight_one,
                jnp.stack([grad_gain_one, grad_shift_one, grad_gain_two, grad_shift_two]),
                jnp.broadcast_to(loss_sum, (1, channels)),
                jnp.broadcast_to(frame_count, (1, channels)),
            ],
            axis=0,
        )

    saved = (misfit, windows, first_unit, grad_gain_two, grad_shift_two)
    if staged:
        half = 3 * channels // groups // 2
        middle = channels // 2
        strides = [1 << bit for bit in range(2, peers.bit_length() - 1)]
        group_strides = [1 << bit for bit in range(groups.bit_length() - 2, -1, -1)]
        patch_bound = channels**0.5 * jnp.max(jnp.abs(first_gain)) + jnp.max(jnp.abs(first_shift))
        bound = jnp.max(jnp.abs(grad_pre.astype(jnp.float32)), axis=0, keepdims=True)
        bound = bound * (later * rows * patch_bound)
        exponent = jnp.ceil(jnp.log2(jnp.maximum(bound, 1e-30)))
        (exponent,) = tie(exponent)

        total = product(patches).reshape(groups, 2, half, channels)
        sent = lax.dynamic_index_in_dim(total, 1 - core, 1, keepdims=False)
        kept = lax.dynamic_index_in_dim(total, core, 1, keepdims=False)
        message = packed(sent.reshape(-1, channels), exponent)
        total, exponent = added(kept.reshape(-1, channels), exponent, swap(message, "dp", 1))

        near, far = total[:, :middle], total[:, middle:]
        near_exponent, far_exponent = exponent[:, :middle], exponent[:, middle:]
        near_message = scatter_message(near, near_exponent, "fsdp", group_strides[0])
        sides = far.reshape(groups, 2, half // 2, middle)
        kept = lax.dynamic_index_in_dim(sides, side, 1, keepdims=False).reshape(-1, middle)
        sent = lax.dynamic_index_in_dim(sides, 1 - side, 1, keepdims=False).reshape(-1, middle)
        far_message = packed(sent, far_exponent)
        grad_pre, near_message, far_message = tie(grad_pre, near_message, far_message)
        small = backward(grad_pre, *saved)
        far, far_exponent = added(kept, far_exponent, swap(far_message, "dp", 2))
        for mask in group_strides:
            if mask != group_strides[0]:
                near_message = scatter_message(near, near_exponent, "fsdp", mask)
            near, near_exponent = scatter_sum(near, near_exponent, near_message, "fsdp", mask)
        near_message = scatter_message(near, near_exponent, "dp", 2)
        far_message = scatter_message(far, far_exponent, "fsdp", group_strides[0])
        small, near_message, far_message = tie(small, near_message, far_message)
        small = small + swap(small, "dp", 1)
        near, near_exponent = scatter_sum(near, near_exponent, near_message, "dp", 2)
        for mask in group_strides:
            if mask != group_strides[0]:
                far_message = scatter_message(far, far_exponent, "fsdp", mask)
            far, far_exponent = scatter_sum(far, far_exponent, far_message, "fsdp", mask)
        total = jnp.concatenate([near, far], axis=1)
        exponent = jnp.concatenate([near_exponent, far_exponent], axis=1)

        steps = [("fsdp", mask) for mask in group_strides] + [("dp", 2)]
        steps += [("dp", mask) for mask in strides]
        for mask in strides:
            message = scatter_message(total, exponent, "dp", mask)
            message, small = tie(message, small)
            axis_name, small_mask = steps.pop(0)
            small = small + swap(small, axis_name, small_mask)
            total, exponent = scatter_sum(total, exponent, message, "dp", mask)
        piece = total.shape[0]
        message = packed(total, exponent)
        for mask in strides[::-1] + [2]:
            message, small = tie(message, small)
            if steps:
                axis_name, small_mask = steps.pop(0)
                small = small + swap(small, axis_name, small_mask)
            message = gather_pair(message, "dp", mask)
        while steps:
            axis_name, small_mask = steps.pop(0)
            small = small + swap(small, axis_name, small_mask)
        other_message = swap(message, "dp", 1)

        def opened(blocks):
            blocks = blocks.reshape(-1, piece + 8, channels)
            (scale,) = tie(jnp.exp2(blocks[:, piece:, :].astype(jnp.float32)[:, :1] - 14.0))
            return (blocks[:, :piece].astype(jnp.float32) * scale).reshape(half, channels)

        gradient = jnp.zeros((2 * half, channels), jnp.float32)
        gradient = lax.dynamic_update_slice_in_dim(gradient, opened(message), core * half, axis=0)
        grad_weight_two = lax.dynamic_update_slice_in_dim(
            gradient, opened(other_message), (1 - core) * half, axis=0
        )
    else:
        partial = lax.psum_scatter(product(patches), "fsdp", scatter_dimension=0, tiled=True)
        grad_weight_two = lax.psum(partial, "dp")
        small = lax.psum(backward(grad_pre, *saved), ("dp", "fsdp"))

    logvar = (raw_logvar * frame_mask).reshape(later, rows).T
    loss = small[14, 0] / small[15, 0]
    return (logvar, loss, grad_weight_two, small[:10], small[10], small[11], small[12], small[13])


def solution(mesh):
    placed = (
        P(("dp", "fsdp"), None),
        P(("dp", "fsdp")),
        P(("dp", "fsdp")),
        P(("dp", "fsdp"), None),
        P(),
        P(),
        P(),
        P("fsdp", None),
        P(),
        P(),
    )
    return jax.shard_map(
        per_device,
        mesh=mesh,
        in_specs=placed,
        out_specs=(P(("dp", "fsdp"), None), P(), P("fsdp", None), P(), P(), P(), P(), P()),
        check_vma=False,
    )
```

```python
import functools

import jax
import jax.numpy as jnp
from jax import lax
from jax.experimental import pallas as pl
from jax.experimental.pallas import tpu as pltpu
from jax.sharding import PartitionSpec as P

epsilon = 1e-05
HIGHEST = lax.Precision.HIGHEST


def tie(*values):
    return lax.optimization_barrier(values)


def power_of_two(value):
    return value & (value - 1) == 0


def swap(values, axis_name, mask):
    size = lax.axis_size(axis_name)
    return lax.ppermute(values, axis_name, [(i, i ^ mask) for i in range(size)])


def part_of(values, index, count):
    size = values.shape[0] // count
    return lax.dynamic_slice_in_dim(values, index * size, size, axis=0)


def scaled_rows(values):
    bound = jnp.max(jnp.abs(values), axis=0, keepdims=True)
    exponent = jnp.ceil(jnp.log2(jnp.maximum(bound, 1e-30)))
    values = values * jnp.exp2(14.0 - exponent)
    upper = lax.reduce_precision(values, 5, 10)
    return jnp.concatenate([upper, (values - upper) * 2048.0], axis=0), exponent


def packed(values, exponent, small=None):
    note = jnp.broadcast_to(exponent, (8, values.shape[1]))
    (scale,) = tie(jnp.exp2(14.0 - exponent))
    parts = [values * scale, note]
    if small is not None:
        rows, small_exponent = scaled_rows(small)
        parts[1] = jnp.where(jnp.arange(8)[:, None] == 0, note, small_exponent)
        parts.append(rows)
    return jnp.concatenate(parts, axis=0).astype(jnp.float16)


def opened_small(message, rows):
    exponent = message[rows : rows + 8].astype(jnp.float32)[1:2]
    parts = message[rows + 8 :].astype(jnp.float32)
    count = parts.shape[0] // 2
    return (parts[:count] + parts[count:] * 2.0**-11) * jnp.exp2(exponent - 14.0)


def exchanged_small(sent, received, rows):
    return opened_small(sent, rows) + opened_small(received, rows)


def opened(message, rows):
    exponent = message[rows : rows + 8].astype(jnp.float32)[:1]
    (scale,) = tie(jnp.exp2(exponent - 14.0))
    return message[:rows].astype(jnp.float32) * scale, exponent


def added(total, exponent, message):
    rows = total.shape[0]
    received = message[rows : rows + 8].astype(jnp.float32)[:1]
    scale, larger = tie(jnp.exp2(received - 14.0), jnp.maximum(received, exponent) + 1.0)
    return total + message[:rows].astype(jnp.float32) * scale, larger


def half_of(total, axis_name, mask, other=False):
    bit = jnp.minimum(lax.axis_index(axis_name) & mask, 1)
    return part_of(total, 1 - bit if other else bit, 2)


def gather_pair(values, received, axis_name, mask):
    bit = jnp.minimum(lax.axis_index(axis_name) & mask, 1)
    size = values.shape[0]
    whole = jnp.zeros((2 * size,) + values.shape[1:], values.dtype)
    whole = lax.dynamic_update_slice_in_dim(whole, values, bit * size, axis=0)
    return lax.dynamic_update_slice_in_dim(whole, received, (1 - bit) * size, axis=0)


def gelu_share(values):
    return 0.5 * lax.erf(values * 0.5**0.5) + 0.5


def gelu_slope(values):
    return gelu_share(values) + values * jnp.exp(-0.5 * values * values) * 0.3989422804014327


def row_mean(values):
    return jnp.sum(values, axis=-1, keepdims=True) * (1.0 / values.shape[-1])


def first_raw(windows, weight):
    return jnp.dot(
        windows[...],
        weight[...],
        precision=HIGHEST,
        preferred_element_type=jnp.float32,
    )


def unit_of(raw):
    centered = raw - row_mean(raw)
    scale = lax.rsqrt(row_mean(centered * centered) + epsilon)
    return centered * scale, scale


def blocks_of(total, size):
    return [slice(start, min(start + size, total)) for start in range(0, total, size)]


def folded(values):
    return jnp.sum(values.reshape(-1, 8, values.shape[-1]), axis=0)


def first_kernel(windows, weight, vectors, act, raw):
    raw[...] = first_raw(windows, weight)
    gains, shifts = vectors[0:1, :], vectors[1:2, :]
    for rows in blocks_of(raw.shape[0], 80):
        normed = unit_of(raw[rows, :])[0] * gains + shifts
        act[rows, :] = (normed * gelu_share(normed)).astype(jnp.bfloat16)


def first_layer(windows, weight, vectors):
    shape = (windows.shape[0], weight.shape[1])
    return pl.pallas_call(
        first_kernel,
        out_shape=jax.ShapeDtypeStruct(shape, jnp.bfloat16),
        scratch_shapes=[pltpu.VMEM(shape, jnp.float32)],
        compiler_params=pltpu.CompilerParams(vmem_limit_bytes=4 << 20),
    )(windows, weight, vectors)


def back_kernel(
    windows, windows_across, first_weight, vectors, weight, padded, sums, small, raw, grad
):
    later_rows = raw.shape[0] - padded.shape[0]
    even_rows, channels = padded.shape
    step = even_rows - later_rows
    raw[...] = first_raw(windows, first_weight)

    def pulled(values, tap):
        return lax.dot_general(
            values,
            weight[tap * channels : (tap + 1) * channels, :],
            (((1,), (1,)), ((), ())),
            preferred_element_type=jnp.float32,
        )

    values = padded[...]
    latest = pulled(values, 2)
    grad[:even_rows, :] = pulled(values, 0)
    grad[step:even_rows, :] += latest[:later_rows]
    grad[even_rows:, :] = pulled(values, 1)[:later_rows]
    gains, shifts = vectors[0:1, :], vectors[1:2, :]
    gain_sum = jnp.zeros((8, channels), jnp.float32)
    shift_sum = jnp.zeros((8, channels), jnp.float32)
    for rows in blocks_of(raw.shape[0], 40):
        unit, scale = unit_of(raw[rows, :])
        grad_out = grad[rows, :] * gelu_slope(unit * gains + shifts)
        grad_unit = grad_out * gains
        grad[rows, :] = scale * (
            grad_unit - row_mean(grad_unit) - unit * row_mean(grad_unit * unit)
        )
        gain_sum += folded(grad_out * unit)
        shift_sum += folded(grad_out)
    taps = windows_across.shape[0]
    small[:taps, :] = jnp.dot(
        windows_across[...], grad[...], precision=HIGHEST, preferred_element_type=jnp.float32
    )
    small[taps : taps + 1, :] = jnp.sum(gain_sum, axis=0, keepdims=True)
    small[taps + 1 : taps + 2, :] = jnp.sum(shift_sum, axis=0, keepdims=True)
    small[taps + 2 :, :] = sums[:4, :]


def backward(windows, windows_across, first_weight, vectors, weight, padded, sums):
    frames, channels = windows.shape[0], vectors.shape[1]
    return pl.pallas_call(
        back_kernel,
        out_shape=jax.ShapeDtypeStruct((windows.shape[1] + 6, channels), jnp.float32),
        scratch_shapes=[pltpu.VMEM((frames, channels), jnp.float32)] * 2,
        compiler_params=pltpu.CompilerParams(vmem_limit_bytes=8 << 20),
    )(windows, windows_across, first_weight, vectors, weight, padded, sums)


def head_kernel(groups, place, act, *refs):
    *weights, target, valid, vectors = refs[:-8]
    weight_out, padded, logvar, sums, message, weight, grad, semaphore = refs[-8:]
    later_rows, channels = target.shape[0], vectors.shape[1]
    even_rows = padded.shape[0]
    step = even_rows - later_rows
    depth = weight.shape[0]
    half = depth // groups // 2
    group, core = place[0], place[1]
    if len(weights) == 1:
        places = [slice(None)]
    else:
        base = (1 - group) * 2 * half
        places = [
            pl.ds(pl.multiple_of(group * 2 * half, half), 2 * half),
            pl.ds(pl.multiple_of(base + core * half, half), half),
            pl.ds(pl.multiple_of(base + (1 - core) * half, half), half),
        ]
    copies = [
        pltpu.make_async_copy(source, weight.at[rows, :], semaphore.at[index])
        for index, (source, rows) in enumerate(zip(weights, places))
    ]
    for copy in copies:
        copy.start()
    for copy in copies:
        copy.wait()
    copy = pltpu.make_async_copy(weight, weight_out, semaphore.at[3])
    copy.start()

    def matmul(left, right):
        return jnp.dot(left, right, preferred_element_type=jnp.float32)

    even, odd = act[:even_rows, :], act[even_rows:, :]
    latest = matmul(even, weight[2 * channels :, :])
    grad[:later_rows, :] = (
        matmul(even, weight[:channels, :])[:later_rows]
        + matmul(odd, weight[channels : 2 * channels, :])
        + latest[step:]
    )
    gains, shifts = vectors[2:3, :], vectors[3:4, :]
    block = 3 * step if later_rows % (3 * step) == 0 else step
    last = jnp.concatenate([valid[...]] * (block // step), axis=0)
    times = lax.broadcasted_iota(jnp.int32, (block, 1), 0)
    gain_sum = jnp.zeros((8, channels), jnp.float32)
    shift_sum = jnp.zeros((8, channels), jnp.float32)
    largest = jnp.zeros((8, channels), jnp.float32)
    loss_sum = jnp.zeros((block, 1), jnp.float32)
    count = jnp.zeros((block, 1), jnp.float32)
    for rows in blocks_of(later_rows, block):
        unit, scale = unit_of(grad[rows, :])
        normed = unit * gains + shifts
        share = gelu_share(normed)
        slope = share + normed * (jnp.exp(-0.5 * normed * normed) * 0.3989422804014327)
        active = normed * share
        active = active - row_mean(active)
        variance = row_mean(active * active) + epsilon
        raw_logvar = jnp.log(variance)
        frame_mask = jnp.where(times + rows.start < last, 1.0, 0.0)
        logvar[rows, :] = raw_logvar * frame_mask
        misfit = raw_logvar - target[rows, :]
        weighted = frame_mask * misfit
        loss_sum += weighted * misfit
        count += frame_mask
        grad_out = weighted / variance * (4.0 / channels) * active * slope
        grad_unit = grad_out * gains
        result = scale * (grad_unit - row_mean(grad_unit) - unit * row_mean(grad_unit * unit))
        gain_sum += folded(grad_out * unit)
        shift_sum += folded(grad_out)
        largest = jnp.maximum(
            largest, jnp.max(jnp.abs(result).reshape(-1, 8, channels), axis=0)
        )
        grad[rows, :] = result
    sums[0:1, :] = jnp.sum(gain_sum, axis=0, keepdims=True)
    sums[1:2, :] = jnp.sum(shift_sum, axis=0, keepdims=True)
    sums[2:3, :] = jnp.broadcast_to(jnp.sum(loss_sum, axis=0, keepdims=True), (1, channels))
    sums[3:4, :] = jnp.broadcast_to(jnp.sum(count, axis=0, keepdims=True), (1, channels))
    sums[4:8, :] = jnp.zeros((4, channels), jnp.float32)
    patch_bound = channels**0.5 * jnp.max(
        jnp.abs(vectors[0:1, :]), axis=1, keepdims=True
    ) + jnp.max(jnp.abs(vectors[1:2, :]), axis=1, keepdims=True)
    grad[later_rows:, :] = jnp.zeros((step, channels), jnp.float32)
    padded[...] = grad[...].astype(jnp.bfloat16)
    bound = jnp.max(largest, axis=0, keepdims=True) * 1.01 * (later_rows * patch_bound)
    exponent = jnp.ceil(jnp.log2(jnp.maximum(bound, 1e-30)))
    sums[8:, :] = jnp.broadcast_to(exponent, (8, channels))
    middle = channels // 2
    away = pl.ds(pl.multiple_of((1 - core) * middle, middle), middle)
    message[:even_rows, :] = grad[:, away].astype(jnp.bfloat16)
    message[even_rows:, :] = sums[8:, away].astype(jnp.bfloat16)
    copy.wait()


def head(groups, place, act, weights, target, valid, vectors):
    channels = act.shape[1]
    depth = 3 * channels
    later_rows = target.shape[0]
    even_rows = act.shape[0] - later_rows
    shapes = [
        pltpu.HBM((depth, channels), jnp.bfloat16),
        pltpu.VMEM((even_rows, channels), jnp.bfloat16),
        pltpu.HBM((later_rows, 1), jnp.float32),
        pltpu.VMEM((16, channels), jnp.float32),
        pltpu.VMEM((even_rows + 8, channels // 2), jnp.bfloat16),
    ]
    weights = [pltpu.with_memory_space_constraint(part, pltpu.HBM) for part in weights]
    arrays = [act, *weights, target, valid, vectors]
    return pl.pallas_call(
        functools.partial(head_kernel, groups),
        out_shape=shapes,
        in_specs=[
            pl.BlockSpec(memory_space=pltpu.SMEM),
            pl.BlockSpec(memory_space=pltpu.VMEM),
        ]
        + [pl.BlockSpec(memory_space=pl.ANY)] * len(weights)
        + [pl.BlockSpec(memory_space=pltpu.VMEM)] * 3,
        out_specs=[pl.BlockSpec(memory_space=pltpu.HBM)]
        + [pl.BlockSpec(memory_space=pltpu.VMEM)] * (len(shapes) - 1),
        scratch_shapes=[
            pltpu.VMEM((depth, channels), jnp.bfloat16),
            pltpu.VMEM((even_rows, channels), jnp.float32),
            pltpu.SemaphoreType.DMA((4,)),
        ],
        compiler_params=pltpu.CompilerParams(vmem_limit_bytes=8 << 20),
    )(place, *arrays)


def split_kernel(
    groups,
    place,
    own_act,
    other_act,
    own_grad,
    received,
    own_note,
    near_message,
    near_kept,
    far_message,
    far_kept,
    note,
    product,
):
    depth, middle = product.shape
    even_rows = own_grad.shape[0]
    later_rows = own_act.shape[0] - even_rows
    step, channels = even_rows - later_rows, own_act.shape[1]
    quarter = middle // 2
    core, bit, side = place[0], place[1], place[2]
    columns = pl.ds(pl.multiple_of(core * middle, middle), middle)

    def outer(left, right):
        return lax.dot_general(
            left, right, (((0,), (0,)), ((), ())), preferred_element_type=jnp.float32
        )

    def shifted(values):
        values = values[:later_rows].astype(jnp.float32)
        zeros = jnp.zeros((step, middle), jnp.float32)
        return jnp.concatenate([zeros, values], axis=0).astype(jnp.bfloat16)

    own, other = own_grad[:, columns], received[:even_rows, :]
    own_even, own_odd = own_act[:even_rows, :], own_act[even_rows:, :]
    other_even, other_odd = other_act[:even_rows, :], other_act[even_rows:, :]
    product[:channels, :] = outer(own_even, own) + outer(other_even, other)
    product[channels : 2 * channels, :] = outer(own_odd, own[:later_rows]) + outer(
        other_odd, other[:later_rows]
    )
    product[2 * channels :, :] = outer(own_even, shifted(own)) + outer(other_even, shifted(other))

    larger = jnp.maximum(own_note[8:, columns], received[even_rows:, :].astype(jnp.float32)) + 1.0
    note[...] = larger
    near, far = slice(0, quarter), slice(quarter, middle)
    stay, size = depth // 2, depth // groups
    cut = size // 2
    near_message[:stay, :] = product[
        pl.ds(pl.multiple_of((1 - bit) * stay, 16), stay), near
    ].astype(jnp.bfloat16)
    near_message[stay:, :] = larger[:, near].astype(jnp.bfloat16)
    far_message[stay:, :] = larger[:, far].astype(jnp.bfloat16)
    for index in range(groups):
        rows = slice(index * cut, (index + 1) * cut)
        away = pl.ds(pl.multiple_of(index * size + (1 - side) * cut, 16), cut)
        far_message[rows, :] = product[away, far].astype(jnp.bfloat16)
        far_kept[rows, :] = product[pl.ds(pl.multiple_of(index * size + side * cut, 16), cut), far]
    near_kept[...] = product[pl.ds(pl.multiple_of(bit * stay, 16), stay), near]


def split(groups, place, own_act, other_act, own_grad, received, note):
    channels = own_act.shape[1]
    depth, quarter = 3 * channels, channels // 4
    message = jax.ShapeDtypeStruct((depth // 2 + 8, quarter), jnp.bfloat16)
    part = jax.ShapeDtypeStruct((depth // 2, quarter), jnp.float32)
    shapes = [message, part, message, part, jax.ShapeDtypeStruct((8, 2 * quarter), jnp.float32)]
    return pl.pallas_call(
        functools.partial(split_kernel, groups),
        out_shape=shapes,
        in_specs=[pl.BlockSpec(memory_space=pltpu.SMEM)]
        + [pl.BlockSpec(memory_space=pltpu.VMEM)] * 5,
        out_specs=[pl.BlockSpec(memory_space=pltpu.VMEM)] * len(shapes),
        scratch_shapes=[pltpu.VMEM((depth, 2 * quarter), jnp.float32)],
        compiler_params=pltpu.CompilerParams(vmem_limit_bytes=8 << 20),
    )(place, own_act, other_act, own_grad, received, note)


def added_plain(total, exponent, message):
    rows = total.shape[0]
    received = message[rows : rows + 8].astype(jnp.float32)[:1]
    (larger,) = tie(jnp.maximum(received, exponent) + 1.0)
    return total + message[:rows].astype(jnp.float32), larger


def per_device(
    waveform,
    lengths,
    owner_of,
    targets,
    first_weight,
    first_gain,
    first_shift,
    second_weight,
    second_gain,
    second_shift,
):
    peers, groups = lax.axis_size("dp"), lax.axis_size("fsdp")
    rows, samples = waveform.shape
    later = targets.shape[1]
    frames = samples // 5 - 1
    channels = first_weight.shape[1]
    staged = power_of_two(peers) and power_of_two(groups) and peers >= 4 and groups > 1
    core, side = lax.axis_index("dp") % 2, lax.axis_index("dp") // 2 % 2

    vectors = jnp.stack([first_gain, first_shift, second_gain, second_shift] * 2)

    fetched = None
    if staged and groups == 2:
        fetched = swap(part_of(second_weight, core, 2), "fsdp", 1)

    width = samples + 1
    noted = jnp.concatenate([waveform, lengths.astype(jnp.float32)[:, None]], axis=1)
    per_owner = max(1, 2 * rows // peers)
    matches = (owner_of[:, None] == owner_of[None, :]).astype(jnp.int32)
    slots = owner_of * per_owner + jnp.sum(jnp.tril(matches, -1), axis=1)
    placing = slots[:, None] == jnp.arange(peers * per_owner, dtype=jnp.int32)[None, :]
    sent = lax.dot_general(
        placing.astype(jnp.float32),
        noted,
        (((0,), (0,)), ((), ())),
        precision=HIGHEST,
        preferred_element_type=jnp.float32,
    )
    got = lax.all_to_all(sent, "dp", split_axis=0, concat_axis=0, tiled=True)
    if fetched is not None:
        got, fetched, vectors = tie(got, fetched, vectors)
        fetched_others = swap(fetched, "dp", 1)
    present = got[:, samples] > 0.5
    arrival = jnp.cumsum(present.astype(jnp.int32)) - 1
    picking = present[None, :] & (
        arrival[None, :] == jnp.arange(rows, dtype=jnp.int32)[:, None]
    )
    owned = jnp.dot(
        picking.astype(jnp.float32), got, precision=HIGHEST, preferred_element_type=jnp.float32
    )
    waveform, lengths = owned[:, :samples], owned[:, samples].astype(jnp.int32)

    blocks = waveform.reshape(rows, later + 1, 2, 5).transpose(1, 2, 0, 3)
    earlier_block, later_block = blocks[:, 0], blocks[:, 1]
    windows = jnp.concatenate(
        [
            jnp.concatenate([earlier_block, later_block], axis=2),
            jnp.concatenate([later_block[:later], earlier_block[1:]], axis=2),
        ],
        axis=0,
    ).reshape(frames * rows, 10)
    if fetched is None:
        weights = [lax.all_gather(second_weight, "fsdp", axis=0, tiled=True)]
    else:
        weights = [second_weight, fetched, fetched_others]
    first = (first_weight, vectors)
    windows_across = windows.T
    act = first_layer(windows, *first)
    if staged:
        act_other = swap(act, "dp", 1)

    first_valid = (lengths - 10) // 5 + 1
    second_valid = ((first_valid - 3) // 2 + 1) * rows
    weight, padded, flat_logvar, sums, message = head(
        groups,
        jnp.stack([lax.axis_index("fsdp"), core]),
        act,
        weights,
        targets.T.reshape(later * rows, 1),
        second_valid[:, None],
        vectors,
    )

    if staged:
        group_rows = 3 * channels // groups
        middle, quarter = channels // 2, channels // 4
        strides = [1 << bit for bit in range(2, peers.bit_length() - 1)]
        group_strides = [1 << bit for bit in range(groups.bit_length() - 2, -1, -1)]
        top = group_strides[0]
        received = swap(message, "dp", 1)
        bit = jnp.minimum(lax.axis_index("fsdp") & top, 1)
        near_message, near, far_message, far, note = split(
            groups, jnp.stack([core, bit, side]), act, act_other, padded, received, sums
        )
        near_exponent, far_exponent = note[:1, :quarter], note[:1, quarter:]
        padded, near_message, far_message = tie(padded, near_message, far_message)
        small = backward(windows, windows_across, *first, weight, padded, sums)
        far, far_exponent = added_plain(far, far_exponent, swap(far_message, "dp", 2))
        received = swap(near_message, "fsdp", top)
        near, near_exponent = added_plain(near, near_exponent, received)
        for mask in group_strides[1:]:
            near_message = packed(half_of(near, "fsdp", mask, True), near_exponent)
            received = swap(near_message, "fsdp", mask)
            near, near_exponent = added(half_of(near, "fsdp", mask), near_exponent, received)
        near_message = packed(half_of(near, "dp", 2, True), near_exponent)
        small = jnp.concatenate(
            [small[:, start : start + quarter] for start in range(0, channels, quarter)], axis=0
        )
        for mask in group_strides:
            sent = half_of(far, "fsdp", mask, True)
            far_message = packed(sent, far_exponent, small)
            near_message, far_message = tie(near_message, far_message)
            received = swap(far_message, "fsdp", mask)
            small = exchanged_small(far_message, received, sent.shape[0])
            far, far_exponent = added(half_of(far, "fsdp", mask), far_exponent, received)
        received = swap(near_message, "dp", 2)
        near, near_exponent = added(half_of(near, "dp", 2), near_exponent, received)
        total = jnp.concatenate([near, far], axis=1)
        exponent = jnp.concatenate([near_exponent, far_exponent], axis=1)
        count = small.shape[0] // 2
        small = jnp.concatenate([small[:count], small[count:]], axis=1)

        for mask in strides[:-1]:
            sent = half_of(total, "dp", mask, True)
            message = packed(sent, exponent, small)
            received = swap(message, "dp", mask)
            small = exchanged_small(message, received, sent.shape[0])
            total, exponent = added(half_of(total, "dp", mask), exponent, received)
        piece = total.shape[0]
        for mask in strides[-1:]:
            message = packed(total, exponent, small)
            received = swap(message, "dp", mask)
            small = exchanged_small(message, received, piece)
            total, exponent = opened(message, piece)
            total, exponent = added(total, exponent, received)
        message = packed(total, exponent)
        small = small + swap(small, "dp", 1)
        for mask in strides[-2::-1]:
            message = gather_pair(message, swap(message, "dp", mask), "dp", mask)

        rows_sent = message.shape[0]
        extra, small_exponent = scaled_rows(small)
        small_exponent = jnp.broadcast_to(small_exponent, (8, middle))
        extra = jnp.concatenate([small_exponent, extra], axis=0)
        sent = jnp.concatenate([message, extra.astype(jnp.float16)], axis=0)
        received = swap(sent, "dp", 2)
        small = exchanged_small(sent, received, rows_sent)
        message = gather_pair(message, received[:rows_sent], "dp", 2)
        other_message = swap(message, "dp", 1)
        count = small.shape[0] // 2
        small = jnp.concatenate(
            [
                small[start : start + count, place : place + quarter]
                for place in (0, quarter)
                for start in (0, count)
            ],
            axis=1,
        )

        def opened_blocks(blocks):
            blocks = blocks.reshape(-1, piece + 8, middle)
            (scale,) = tie(jnp.exp2(blocks[:, piece:, :].astype(jnp.float32)[:, :1] - 14.0))
            return (blocks[:, :piece].astype(jnp.float32) * scale).reshape(group_rows, middle)

        gradient = jnp.zeros((group_rows, channels), jnp.float32)
        gradient = lax.dynamic_update_slice_in_dim(
            gradient, opened_blocks(message), core * middle, axis=1
        )
        grad_weight_two = lax.dynamic_update_slice_in_dim(
            gradient, opened_blocks(other_message), (1 - core) * middle, axis=1
        )
    else:
        even, odd = act[: padded.shape[0]], act[padded.shape[0] :]
        zeros = jnp.zeros((rows, channels), padded.dtype)
        shifted = jnp.concatenate([zeros, padded[: later * rows]], axis=0)
        pairs = [(even, padded), (odd, padded[: later * rows]), (even, shifted)]
        partial = [
            lax.dot_general(
                left, right, (((0,), (0,)), ((), ())), preferred_element_type=jnp.float32
            )
            for left, right in pairs
        ]
        partial = jnp.concatenate(partial, axis=0)
        partial = lax.psum_scatter(partial, "fsdp", scatter_dimension=0, tiled=True)
        grad_weight_two = lax.psum(partial, "dp")
        small = backward(windows, windows_across, *first, weight, padded, sums)
        small = lax.psum(small, ("dp", "fsdp"))

    logvar = flat_logvar.reshape(later, rows).T
    loss = small[14, 0] / small[15, 0]
    return (logvar, loss, grad_weight_two, small[:10], small[10], small[11], small[12], small[13])


def solution(mesh):
    placed = (
        P(("dp", "fsdp"), None),
        P(("dp", "fsdp")),
        P(("dp", "fsdp")),
        P(("dp", "fsdp"), None),
        P(),
        P(),
        P(),
        P("fsdp", None),
        P(),
        P(),
    )
    return jax.shard_map(
        per_device,
        mesh=mesh,
        in_specs=placed,
        out_specs=(P(("dp", "fsdp"), None), P(), P("fsdp", None), P(), P(), P(), P(), P()),
        check_vma=False,
    )
```

```python
import functools

import jax
import jax.numpy as jnp
from jax import lax
from jax.experimental import pallas as pl
from jax.experimental.pallas import tpu as pltpu
from jax.sharding import PartitionSpec as P


epsilon = 1e-05
HIGHEST = lax.Precision.HIGHEST


def tie(*values):
    return lax.optimization_barrier(values)


def power_of_two(value):
    return value & (value - 1) == 0


def swap(values, axis_name, mask):
    size = lax.axis_size(axis_name)
    return lax.ppermute(values, axis_name, [(i, i ^ mask) for i in range(size)])


def part_of(values, index, count):
    size = values.shape[0] // count
    return lax.dynamic_slice_in_dim(values, index * size, size, axis=0)


def scaled_rows(values):
    bound = jnp.max(jnp.abs(values), axis=0, keepdims=True)
    exponent = jnp.ceil(jnp.log2(jnp.maximum(bound, 1e-30)))
    values = values * jnp.exp2(14.0 - exponent)
    upper = lax.reduce_precision(values, 5, 10)
    return jnp.concatenate([upper, (values - upper) * 2048.0], axis=0), exponent


def packed(values, exponent, small=None):
    note = jnp.broadcast_to(exponent, (8, values.shape[1]))
    (scale,) = tie(jnp.exp2(14.0 - exponent))
    parts = [values * scale, note]
    if small is not None:
        rows, small_exponent = scaled_rows(small)
        parts[1] = jnp.where(jnp.arange(8)[:, None] == 0, note, small_exponent)
        parts.append(rows)
    return jnp.concatenate(parts, axis=0).astype(jnp.float16)


def opened_small(message, rows):
    exponent = message[rows : rows + 8].astype(jnp.float32)[1:2]
    parts = message[rows + 8 :].astype(jnp.float32)
    count = parts.shape[0] // 2
    return (parts[:count] + parts[count:] * 2.0**-11) * jnp.exp2(exponent - 14.0)


def exchanged_small(sent, received, rows):
    return opened_small(sent, rows) + opened_small(received, rows)


def opened(message, rows):
    exponent = message[rows : rows + 8].astype(jnp.float32)[:1]
    (scale,) = tie(jnp.exp2(exponent - 14.0))
    return message[:rows].astype(jnp.float32) * scale, exponent


def added(total, exponent, message):
    rows = total.shape[0]
    received = message[rows : rows + 8].astype(jnp.float32)[:1]
    scale, larger = tie(jnp.exp2(received - 14.0), jnp.maximum(received, exponent) + 1.0)
    return total + message[:rows].astype(jnp.float32) * scale, larger


def half_of(total, axis_name, mask, other=False):
    bit = jnp.minimum(lax.axis_index(axis_name) & mask, 1)
    return part_of(total, 1 - bit if other else bit, 2)


def gather_pair(values, received, axis_name, mask):
    bit = jnp.minimum(lax.axis_index(axis_name) & mask, 1)
    size = values.shape[0]
    whole = jnp.zeros((2 * size,) + values.shape[1:], values.dtype)
    whole = lax.dynamic_update_slice_in_dim(whole, values, bit * size, axis=0)
    return lax.dynamic_update_slice_in_dim(whole, received, (1 - bit) * size, axis=0)


def gelu_share(values):
    return 0.5 * lax.erf(values * 0.5**0.5) + 0.5


def gelu_slope(values):
    return gelu_share(values) + values * jnp.exp(-0.5 * values * values) * 0.3989422804014327


def row_mean(values):
    return jnp.sum(values, axis=-1, keepdims=True) * (1.0 / values.shape[-1])


def placing_kernel(per_owner, owners_in, lengths_in, waveform_in, weight, out, *refs):
    *pieces, owners, lengths, waveform, semaphores = refs
    copies = [
        pltpu.make_async_copy(owners_in, owners, semaphores.at[0]),
        pltpu.make_async_copy(lengths_in, lengths, semaphores.at[1]),
        pltpu.make_async_copy(waveform_in, waveform, semaphores.at[2]),
    ]
    for piece in pieces:
        size = piece.shape[0]
        start = pl.multiple_of(lax.rem(lax.axis_index("dp"), 2) * size, size)
        copies.append(
            pltpu.make_async_copy(weight.at[pl.ds(start, size), :], piece, semaphores.at[3])
        )
    for copy in copies:
        copy.start()
    samples, width = waveform.shape[1], out.shape[2]
    out[...] = jnp.zeros_like(out)
    for copy in copies[:3]:
        copy.wait()
    for row in range(waveform.shape[0]):
        slot = owners[row] * per_owner
        for earlier in range(row if per_owner > 1 else 0):
            slot += jnp.where(owners[earlier] == owners[row], 1, 0)
        out[slot, :, :samples] = waveform[row : row + 1, :]
        length = lengths[row].astype(jnp.float32)
        out[slot, :, width - 128 :] = jnp.full((1, 128), length, jnp.float32)
    for copy in copies[3:]:
        copy.wait()


def placed_rows(owners, lengths, waveform, weight, peers, halved):
    rows, samples = waveform.shape
    per_owner = max(1, 2 * rows // peers)
    width = -(-samples // 128) * 128 + 128
    shapes = [jax.ShapeDtypeStruct((peers * per_owner, 1, width), jnp.float32)]
    if halved:
        shapes.append(jax.ShapeDtypeStruct((weight.shape[0] // 2, weight.shape[1]), weight.dtype))
    arrays = [
        pltpu.with_memory_space_constraint(array, pltpu.HBM)
        for array in (owners, lengths, waveform, weight)
    ]
    return pl.pallas_call(
        functools.partial(placing_kernel, per_owner),
        out_shape=shapes,
        in_specs=[pl.BlockSpec(memory_space=pl.ANY)] * 4,
        out_specs=[pl.BlockSpec(memory_space=pltpu.VMEM)] * len(shapes),
        scratch_shapes=[
            pltpu.SMEM((rows,), jnp.int32),
            pltpu.SMEM((rows,), jnp.int32),
            pltpu.VMEM((rows, samples), jnp.float32),
            pltpu.SemaphoreType.DMA((4,)),
        ],
        compiler_params=pltpu.CompilerParams(vmem_limit_bytes=3 << 20),
    )(*arrays)


def first_raw(windows, weight):
    return jnp.dot(
        windows[...],
        weight[...],
        precision=HIGHEST,
        preferred_element_type=jnp.float32,
    )


def unit_of(raw):
    centered = raw - row_mean(raw)
    scale = lax.rsqrt(row_mean(centered * centered) + epsilon)
    return centered * scale, scale


def blocks_of(total, size):
    return [slice(start, min(start + size, total)) for start in range(0, total, size)]


def folded(values):
    return jnp.sum(values.reshape(-1, 8, values.shape[-1]), axis=0)


def first_kernel(windows, weight, vectors, act, raw):
    raw[...] = first_raw(windows, weight)
    gains, shifts = vectors[0:1, :], vectors[1:2, :]
    for rows in blocks_of(raw.shape[0], 80):
        normed = unit_of(raw[rows, :])[0] * gains + shifts
        act[rows, :] = (normed * gelu_share(normed)).astype(jnp.bfloat16)


def first_layer(windows, weight, vectors):
    shape = (windows.shape[0], weight.shape[1])
    return pl.pallas_call(
        first_kernel,
        out_shape=jax.ShapeDtypeStruct(shape, jnp.bfloat16),
        scratch_shapes=[pltpu.VMEM(shape, jnp.float32)],
        compiler_params=pltpu.CompilerParams(vmem_limit_bytes=4 << 20),
    )(windows, weight, vectors)


def back_kernel(
    windows, windows_across, first_weight, vectors, weight, padded, sums, small, raw, grad
):
    later_rows = raw.shape[0] - padded.shape[0]
    even_rows, channels = padded.shape
    step = even_rows - later_rows
    raw[...] = first_raw(windows, first_weight)

    def pulled(values, tap):
        return lax.dot_general(
            values,
            weight[tap * channels : (tap + 1) * channels, :],
            (((1,), (1,)), ((), ())),
            preferred_element_type=jnp.float32,
        )

    values = padded[...]
    latest = pulled(values, 2)
    grad[:even_rows, :] = pulled(values, 0)
    grad[step:even_rows, :] += latest[:later_rows]
    grad[even_rows:, :] = pulled(values, 1)[:later_rows]
    gains, shifts = vectors[0:1, :], vectors[1:2, :]
    gain_sum = jnp.zeros((8, channels), jnp.float32)
    shift_sum = jnp.zeros((8, channels), jnp.float32)
    for rows in blocks_of(raw.shape[0], 40):
        unit, scale = unit_of(raw[rows, :])
        grad_out = grad[rows, :] * gelu_slope(unit * gains + shifts)
        grad_unit = grad_out * gains
        grad[rows, :] = scale * (
            grad_unit - row_mean(grad_unit) - unit * row_mean(grad_unit * unit)
        )
        gain_sum += folded(grad_out * unit)
        shift_sum += folded(grad_out)
    taps = windows_across.shape[0]
    small[:taps, :] = jnp.dot(
        windows_across[...], grad[...], precision=HIGHEST, preferred_element_type=jnp.float32
    )
    small[taps : taps + 1, :] = jnp.sum(gain_sum, axis=0, keepdims=True)
    small[taps + 1 : taps + 2, :] = jnp.sum(shift_sum, axis=0, keepdims=True)
    small[taps + 2 :, :] = sums[:4, :]


def backward(windows, windows_across, first_weight, vectors, weight, padded, sums):
    frames, channels = windows.shape[0], vectors.shape[1]
    return pl.pallas_call(
        back_kernel,
        out_shape=jax.ShapeDtypeStruct((windows.shape[1] + 6, channels), jnp.float32),
        scratch_shapes=[pltpu.VMEM((frames, channels), jnp.float32)] * 2,
        compiler_params=pltpu.CompilerParams(vmem_limit_bytes=8 << 20),
    )(windows, windows_across, first_weight, vectors, weight, padded, sums)


def head_kernel(groups, place, act, *refs):
    *weights, target, valid, vectors = refs[:-8]
    weight_out, padded, logvar, sums, message, weight, grad, semaphore = refs[-8:]
    later_rows, channels = target.shape[0], vectors.shape[1]
    even_rows = padded.shape[0]
    step = even_rows - later_rows
    depth = weight.shape[0]
    half = depth // groups // 2
    group, core = place[0], place[1]
    if len(weights) == 1:
        places = [slice(None)]
    else:
        base = (1 - group) * 2 * half
        places = [
            pl.ds(pl.multiple_of(group * 2 * half, half), 2 * half),
            pl.ds(pl.multiple_of(base + core * half, half), half),
            pl.ds(pl.multiple_of(base + (1 - core) * half, half), half),
        ]
    copies = [
        pltpu.make_async_copy(source, weight.at[rows, :], semaphore.at[index])
        for index, (source, rows) in enumerate(zip(weights, places))
    ]
    for copy in copies:
        copy.start()
    for copy in copies:
        copy.wait()
    copy = pltpu.make_async_copy(weight, weight_out, semaphore.at[3])
    copy.start()

    def matmul(left, right):
        return jnp.dot(left, right, preferred_element_type=jnp.float32)

    even, odd = act[:even_rows, :], act[even_rows:, :]
    latest = matmul(even, weight[2 * channels :, :])
    grad[:later_rows, :] = (
        matmul(even, weight[:channels, :])[:later_rows]
        + matmul(odd, weight[channels : 2 * channels, :])
        + latest[step:]
    )
    gains, shifts = vectors[2:3, :], vectors[3:4, :]
    block = 3 * step if later_rows % (3 * step) == 0 else step
    last = jnp.concatenate([valid[...]] * (block // step), axis=0)
    times = lax.broadcasted_iota(jnp.int32, (block, 1), 0)
    gain_sum = jnp.zeros((8, channels), jnp.float32)
    shift_sum = jnp.zeros((8, channels), jnp.float32)
    largest = jnp.zeros((8, channels), jnp.float32)
    loss_sum = jnp.zeros((block, 1), jnp.float32)
    count = jnp.zeros((block, 1), jnp.float32)
    for rows in blocks_of(later_rows, block):
        unit, scale = unit_of(grad[rows, :])
        normed = unit * gains + shifts
        share = gelu_share(normed)
        slope = share + normed * (jnp.exp(-0.5 * normed * normed) * 0.3989422804014327)
        active = normed * share
        active = active - row_mean(active)
        variance = row_mean(active * active) + epsilon
        raw_logvar = jnp.log(variance)
        frame_mask = jnp.where(times + rows.start < last, 1.0, 0.0)
        logvar[rows, :] = raw_logvar * frame_mask
        misfit = raw_logvar - target[rows, :]
        weighted = frame_mask * misfit
        loss_sum += weighted * misfit
        count += frame_mask
        grad_out = weighted / variance * (4.0 / channels) * active * slope
        grad_unit = grad_out * gains
        result = scale * (grad_unit - row_mean(grad_unit) - unit * row_mean(grad_unit * unit))
        gain_sum += folded(grad_out * unit)
        shift_sum += folded(grad_out)
        largest = jnp.maximum(
            largest, jnp.max(jnp.abs(result).reshape(-1, 8, channels), axis=0)
        )
        grad[rows, :] = result
    sums[0:1, :] = jnp.sum(gain_sum, axis=0, keepdims=True)
    sums[1:2, :] = jnp.sum(shift_sum, axis=0, keepdims=True)
    sums[2:3, :] = jnp.broadcast_to(jnp.sum(loss_sum, axis=0, keepdims=True), (1, channels))
    sums[3:4, :] = jnp.broadcast_to(jnp.sum(count, axis=0, keepdims=True), (1, channels))
    sums[4:8, :] = jnp.zeros((4, channels), jnp.float32)
    patch_bound = channels**0.5 * jnp.max(
        jnp.abs(vectors[0:1, :]), axis=1, keepdims=True
    ) + jnp.max(jnp.abs(vectors[1:2, :]), axis=1, keepdims=True)
    grad[later_rows:, :] = jnp.zeros((step, channels), jnp.float32)
    padded[...] = grad[...].astype(jnp.bfloat16)
    bound = jnp.max(largest, axis=0, keepdims=True) * 1.01 * (later_rows * patch_bound)
    exponent = jnp.ceil(jnp.log2(jnp.maximum(bound, 1e-30)))
    sums[8:, :] = jnp.broadcast_to(exponent, (8, channels))
    middle = channels // 2
    away = pl.ds(pl.multiple_of((1 - core) * middle, middle), middle)
    message[:even_rows, :] = grad[:, away].astype(jnp.bfloat16)
    message[even_rows:, :] = sums[8:, away].astype(jnp.bfloat16)
    copy.wait()


def head(groups, place, act, weights, target, valid, vectors):
    channels = act.shape[1]
    depth = 3 * channels
    later_rows = target.shape[0]
    even_rows = act.shape[0] - later_rows
    shapes = [
        pltpu.HBM((depth, channels), jnp.bfloat16),
        pltpu.VMEM((even_rows, channels), jnp.bfloat16),
        pltpu.HBM((later_rows, 1), jnp.float32),
        pltpu.VMEM((16, channels), jnp.float32),
        pltpu.VMEM((even_rows + 8, channels // 2), jnp.bfloat16),
    ]
    weights = [pltpu.with_memory_space_constraint(part, pltpu.HBM) for part in weights]
    arrays = [act, *weights, target, valid, vectors]
    return pl.pallas_call(
        functools.partial(head_kernel, groups),
        out_shape=shapes,
        in_specs=[
            pl.BlockSpec(memory_space=pltpu.SMEM),
            pl.BlockSpec(memory_space=pltpu.VMEM),
        ]
        + [pl.BlockSpec(memory_space=pl.ANY)] * len(weights)
        + [pl.BlockSpec(memory_space=pltpu.VMEM)] * 3,
        out_specs=[pl.BlockSpec(memory_space=pltpu.HBM)]
        + [pl.BlockSpec(memory_space=pltpu.VMEM)] * (len(shapes) - 1),
        scratch_shapes=[
            pltpu.VMEM((depth, channels), jnp.bfloat16),
            pltpu.VMEM((even_rows, channels), jnp.float32),
            pltpu.SemaphoreType.DMA((4,)),
        ],
        compiler_params=pltpu.CompilerParams(vmem_limit_bytes=8 << 20),
    )(place, *arrays)


def split_kernel(
    groups,
    place,
    own_act,
    other_act,
    own_grad,
    received,
    own_note,
    near_message,
    near_kept,
    far_message,
    far_kept,
    note,
    product,
):
    depth, middle = product.shape
    even_rows = own_grad.shape[0]
    later_rows = own_act.shape[0] - even_rows
    step, channels = even_rows - later_rows, own_act.shape[1]
    quarter = middle // 2
    core, bit, side = place[0], place[1], place[2]
    columns = pl.ds(pl.multiple_of(core * middle, middle), middle)

    def outer(left, right):
        return lax.dot_general(
            left, right, (((0,), (0,)), ((), ())), preferred_element_type=jnp.float32
        )

    def shifted(values):
        values = values[:later_rows].astype(jnp.float32)
        zeros = jnp.zeros((step, middle), jnp.float32)
        return jnp.concatenate([zeros, values], axis=0).astype(jnp.bfloat16)

    own, other = own_grad[:, columns], received[:even_rows, :]
    own_even, own_odd = own_act[:even_rows, :], own_act[even_rows:, :]
    other_even, other_odd = other_act[:even_rows, :], other_act[even_rows:, :]
    product[:channels, :] = outer(own_even, own) + outer(other_even, other)
    product[channels : 2 * channels, :] = outer(own_odd, own[:later_rows]) + outer(
        other_odd, other[:later_rows]
    )
    product[2 * channels :, :] = outer(own_even, shifted(own)) + outer(other_even, shifted(other))

    larger = jnp.maximum(own_note[8:, columns], received[even_rows:, :].astype(jnp.float32)) + 1.0
    note[...] = larger
    near, far = slice(0, quarter), slice(quarter, middle)
    stay, size = depth // 2, depth // groups
    cut = size // 2
    near_message[:stay, :] = product[
        pl.ds(pl.multiple_of((1 - bit) * stay, 16), stay), near
    ].astype(jnp.bfloat16)
    near_message[stay:, :] = larger[:, near].astype(jnp.bfloat16)
    far_message[stay:, :] = larger[:, far].astype(jnp.bfloat16)
    for index in range(groups):
        rows = slice(index * cut, (index + 1) * cut)
        away = pl.ds(pl.multiple_of(index * size + (1 - side) * cut, 16), cut)
        far_message[rows, :] = product[away, far].astype(jnp.bfloat16)
        far_kept[rows, :] = product[pl.ds(pl.multiple_of(index * size + side * cut, 16), cut), far]
    near_kept[...] = product[pl.ds(pl.multiple_of(bit * stay, 16), stay), near]


def split(groups, place, own_act, other_act, own_grad, received, note):
    channels = own_act.shape[1]
    depth, quarter = 3 * channels, channels // 4
    message = jax.ShapeDtypeStruct((depth // 2 + 8, quarter), jnp.bfloat16)
    part = jax.ShapeDtypeStruct((depth // 2, quarter), jnp.float32)
    shapes = [message, part, message, part, jax.ShapeDtypeStruct((8, 2 * quarter), jnp.float32)]
    return pl.pallas_call(
        functools.partial(split_kernel, groups),
        out_shape=shapes,
        in_specs=[pl.BlockSpec(memory_space=pltpu.SMEM)]
        + [pl.BlockSpec(memory_space=pltpu.VMEM)] * 5,
        out_specs=[pl.BlockSpec(memory_space=pltpu.VMEM)] * len(shapes),
        scratch_shapes=[pltpu.VMEM((depth, 2 * quarter), jnp.float32)],
        compiler_params=pltpu.CompilerParams(vmem_limit_bytes=8 << 20),
    )(place, own_act, other_act, own_grad, received, note)


def storing_kernel(last, flips, *refs):
    own, other, out, semaphores = refs[-4:]
    me = lax.axis_index("dp")
    core, side, bit = lax.rem(me, 2), lax.rem(me // 2, 2), lax.rem(me // last, 2)
    size, middle = out.shape[0] // 4, own.shape[1]
    copies = []
    for index, (side_flip, bit_flip) in enumerate(flips):
        block = (side + side_flip - 2 * side * side_flip) * 2 + (bit + bit_flip - 2 * bit * bit_flip)
        rows = pl.ds(pl.multiple_of(block * size, 8), size)
        for number, (source, column) in enumerate(((own, core), (other, 1 - core))):
            columns = pl.ds(pl.multiple_of(column * middle, middle), middle)
            copies.append(
                pltpu.make_async_copy(
                    source.at[index * size : (index + 1) * size, :],
                    out.at[rows, columns],
                    semaphores.at[2 * index + number],
                )
            )
    for copy in copies:
        copy.start()
    for copy in copies:
        copy.wait()


def stored(last, flips, shape, before, own, other):
    blocks = [pl.BlockSpec(memory_space=pltpu.VMEM)] * 2
    return pl.pallas_call(
        functools.partial(storing_kernel, last, flips),
        out_shape=pltpu.HBM(shape, jnp.float32),
        in_specs=[pl.BlockSpec(memory_space=pl.ANY)] * len(before) + blocks,
        out_specs=pl.BlockSpec(memory_space=pl.ANY),
        scratch_shapes=[pltpu.SemaphoreType.DMA((2 * len(flips),))],
        input_output_aliases={0: 0} if before else {},
        compiler_params=pltpu.CompilerParams(vmem_limit_bytes=3 << 20),
    )(*before, own, other)


def added_plain(total, exponent, message):
    rows = total.shape[0]
    received = message[rows : rows + 8].astype(jnp.float32)[:1]
    (larger,) = tie(jnp.maximum(received, exponent) + 1.0)
    return total + message[:rows].astype(jnp.float32), larger


def per_device(
    waveform,
    lengths,
    owner_of,
    targets,
    first_weight,
    first_gain,
    first_shift,
    second_weight,
    second_gain,
    second_shift,
):
    peers, groups = lax.axis_size("dp"), lax.axis_size("fsdp")
    rows, samples = waveform.shape
    later = targets.shape[1]
    frames = samples // 5 - 1
    channels = first_weight.shape[1]
    staged = power_of_two(peers) and power_of_two(groups) and peers >= 16 and groups > 1
    core, side = lax.axis_index("dp") % 2, lax.axis_index("dp") // 2 % 2

    vectors = jnp.stack([first_gain, first_shift, second_gain, second_shift] * 2)

    fetched = None
    if staged and groups == 2:
        sent, fetched = placed_rows(owner_of, lengths, waveform, second_weight, peers, True)
        fetched = swap(fetched, "fsdp", 1)
    else:
        (sent,) = placed_rows(owner_of, lengths, waveform, second_weight, peers, False)
    got = lax.all_to_all(sent, "dp", split_axis=0, concat_axis=0, tiled=True)
    got = got.reshape(sent.shape[0], sent.shape[2])
    if fetched is not None:
        got, fetched, vectors = tie(got, fetched, vectors)
        fetched_others = swap(fetched, "dp", 1)
    present = got[:, -1] > 0.5
    arrival = jnp.cumsum(present.astype(jnp.int32)) - 1
    picking = present[None, :] & (
        arrival[None, :] == jnp.arange(rows, dtype=jnp.int32)[:, None]
    )
    waveform = jnp.dot(
        picking.astype(jnp.float32),
        got[:, :samples],
        precision=HIGHEST,
        preferred_element_type=jnp.float32,
    )
    lengths = jnp.sum(jnp.where(picking, got[:, -1][None, :], 0.0), axis=1).astype(jnp.int32)

    blocks = waveform.reshape(rows, later + 1, 2, 5).transpose(1, 2, 0, 3)
    earlier_block, later_block = blocks[:, 0], blocks[:, 1]
    windows = jnp.concatenate(
        [
            jnp.concatenate([earlier_block, later_block], axis=2),
            jnp.concatenate([later_block[:later], earlier_block[1:]], axis=2),
        ],
        axis=0,
    ).reshape(frames * rows, 10)
    if fetched is None:
        weights = [lax.all_gather(second_weight, "fsdp", axis=0, tiled=True)]
    else:
        weights = [second_weight, fetched, fetched_others]
    first = (first_weight, vectors)
    windows_across = windows.T
    act = first_layer(windows, *first)
    if staged:
        act_other = swap(act, "dp", 1)

    first_valid = (lengths - 10) // 5 + 1
    second_valid = ((first_valid - 3) // 2 + 1) * rows
    weight, padded, flat_logvar, sums, message = head(
        groups,
        jnp.stack([lax.axis_index("fsdp"), core]),
        act,
        weights,
        targets.T.reshape(later * rows, 1),
        second_valid[:, None],
        vectors,
    )

    if staged:
        group_rows = 3 * channels // groups
        middle, quarter = channels // 2, channels // 4
        strides = [1 << bit for bit in range(2, peers.bit_length() - 1)]
        group_strides = [1 << bit for bit in range(groups.bit_length() - 2, -1, -1)]
        top = group_strides[0]
        received = swap(message, "dp", 1)
        bit = jnp.minimum(lax.axis_index("fsdp") & top, 1)
        near_message, near, far_message, far, note = split(
            groups, jnp.stack([core, bit, side]), act, act_other, padded, received, sums
        )
        near_exponent, far_exponent = note[:1, :quarter], note[:1, quarter:]
        padded, near_message, far_message = tie(padded, near_message, far_message)
        small = backward(windows, windows_across, *first, weight, padded, sums)
        far, far_exponent = added_plain(far, far_exponent, swap(far_message, "dp", 2))
        received = swap(near_message, "fsdp", top)
        near, near_exponent = added_plain(near, near_exponent, received)
        for mask in group_strides[1:]:
            near_message = packed(half_of(near, "fsdp", mask, True), near_exponent)
            received = swap(near_message, "fsdp", mask)
            near, near_exponent = added(half_of(near, "fsdp", mask), near_exponent, received)
        near_message = packed(half_of(near, "dp", 2, True), near_exponent)
        small = jnp.concatenate(
            [small[:, start : start + quarter] for start in range(0, channels, quarter)], axis=0
        )
        for mask in group_strides:
            sent = half_of(far, "fsdp", mask, True)
            far_message = packed(sent, far_exponent, small)
            near_message, far_message = tie(near_message, far_message)
            received = swap(far_message, "fsdp", mask)
            small = exchanged_small(far_message, received, sent.shape[0])
            far, far_exponent = added(half_of(far, "fsdp", mask), far_exponent, received)
        received = swap(near_message, "dp", 2)
        near, near_exponent = added(half_of(near, "dp", 2), near_exponent, received)
        total = jnp.concatenate([near, far], axis=1)
        exponent = jnp.concatenate([near_exponent, far_exponent], axis=1)
        count = small.shape[0] // 2
        small = jnp.concatenate([small[:count], small[count:]], axis=1)

        for mask in strides[:-1]:
            sent = half_of(total, "dp", mask, True)
            message = packed(sent, exponent, small)
            received = swap(message, "dp", mask)
            small = exchanged_small(message, received, sent.shape[0])
            total, exponent = added(half_of(total, "dp", mask), exponent, received)
        piece = total.shape[0]
        for mask in strides[-1:]:
            message = packed(total, exponent, small)
            received = swap(message, "dp", mask)
            small = exchanged_small(message, received, piece)
            total, exponent = opened(message, piece)
            total, exponent = added(total, exponent, received)
        message = packed(total, exponent)
        for mask in strides[-2:0:-1]:
            message = gather_pair(message, swap(message, "dp", mask), "dp", mask)

        last = strides[0]
        rows_sent = message.shape[0]

        def extended(message, small):
            extra, exponent = scaled_rows(small)
            exponent = jnp.broadcast_to(exponent, (8, middle))
            extra = jnp.concatenate([exponent, extra], axis=0).astype(jnp.float16)
            return jnp.concatenate([message, extra], axis=0)

        sent = extended(message, small)
        received = swap(sent, "dp", 2)
        beside = swap(message, "dp", last)
        small = exchanged_small(sent, received, rows_sent)
        across = received[:rows_sent]
        cut = rows_sent // 16 * 8
        upper = swap(beside[:cut], "dp", 2)
        lower = swap(across[cut:], "dp", last)
        early = jnp.concatenate([message, beside, across], axis=0)
        sent = extended(early, small)
        received = swap(sent, "dp", 1)
        small = exchanged_small(sent, received, early.shape[0])
        early_other = received[: early.shape[0]]
        corner = jnp.concatenate([upper, lower], axis=0)
        count = small.shape[0] // 2
        small = jnp.concatenate(
            [
                small[start : start + count, place : place + quarter]
                for place in (0, quarter)
                for start in (0, count)
            ],
            axis=1,
        )

        def opened_blocks(blocks):
            blocks = blocks.reshape(-1, piece + 8, middle)
            (scale,) = tie(jnp.exp2(blocks[:, piece:, :].astype(jnp.float32)[:, :1] - 14.0))
            return (blocks[:, :piece].astype(jnp.float32) * scale).reshape(-1, middle)

        shape = (group_rows, channels)
        flips = ((0, 0), (0, 1), (1, 0))
        gradient = stored(last, flips, shape, (), opened_blocks(early), opened_blocks(early_other))
        corner, gradient = tie(corner, gradient)
        corner_other = swap(corner, "dp", 1)
        grad_weight_two = stored(
            last, ((1, 1),), shape, (gradient,), opened_blocks(corner), opened_blocks(corner_other)
        )
    else:
        even, odd = act[: padded.shape[0]], act[padded.shape[0] :]
        zeros = jnp.zeros((rows, channels), padded.dtype)
        shifted = jnp.concatenate([zeros, padded[: later * rows]], axis=0)
        pairs = [(even, padded), (odd, padded[: later * rows]), (even, shifted)]
        partial = [
            lax.dot_general(
                left, right, (((0,), (0,)), ((), ())), preferred_element_type=jnp.float32
            )
            for left, right in pairs
        ]
        partial = jnp.concatenate(partial, axis=0)
        partial = lax.psum_scatter(partial, "fsdp", scatter_dimension=0, tiled=True)
        grad_weight_two = lax.psum(partial, "dp")
        small = backward(windows, windows_across, *first, weight, padded, sums)
        small = lax.psum(small, ("dp", "fsdp"))

    logvar = flat_logvar.reshape(later, rows).T
    (loss,) = tie(small[14:15] / small[15:16])
    loss = loss[0, 0]
    return (logvar, loss, grad_weight_two, small[:10], small[10], small[11], small[12], small[13])


def solution(mesh):
    placed = (
        P(("dp", "fsdp"), None),
        P(("dp", "fsdp")),
        P(("dp", "fsdp")),
        P(("dp", "fsdp"), None),
        P(),
        P(),
        P(),
        P("fsdp", None),
        P(),
        P(),
    )

    return jax.shard_map(
        per_device,
        mesh=mesh,
        in_specs=placed,
        out_specs=(P(("dp", "fsdp"), None), P(), P("fsdp", None), P(), P(), P(), P(), P()),
        check_vma=False,
    )
```

```python
import functools

import jax
import jax.numpy as jnp
from jax import lax
from jax.experimental import pallas as pl
from jax.experimental.pallas import tpu as pltpu
from jax.sharding import PartitionSpec as P


epsilon = 1e-05
HIGHEST = lax.Precision.HIGHEST


def tie(*values):
    return lax.optimization_barrier(values)


def power_of_two(value):
    return value & (value - 1) == 0


def swap(values, axis_name, mask):
    size = lax.axis_size(axis_name)
    return lax.ppermute(values, axis_name, [(i, i ^ mask) for i in range(size)])


def part_of(values, index, count):
    size = values.shape[0] // count
    return lax.dynamic_slice_in_dim(values, index * size, size, axis=0)


def scaled_rows(values):
    bound = jnp.max(jnp.abs(values), axis=0, keepdims=True)
    exponent = jnp.ceil(jnp.log2(jnp.maximum(bound, 1e-30)))
    values = values * jnp.exp2(14.0 - exponent)
    upper = lax.reduce_precision(values, 5, 10)
    return jnp.concatenate([upper, (values - upper) * 2048.0], axis=0), exponent


def packed(values, exponent, small=None):
    note = jnp.broadcast_to(exponent, (8, values.shape[1]))
    (scale,) = tie(jnp.exp2(14.0 - exponent))
    parts = [values * scale, note]
    if small is not None:
        rows, small_exponent = scaled_rows(small)
        parts[1] = jnp.where(jnp.arange(8)[:, None] == 0, note, small_exponent)
        parts.append(rows)
    return jnp.concatenate(parts, axis=0).astype(jnp.float16)


def opened_small(message, rows):
    exponent = message[rows : rows + 8].astype(jnp.float32)[1:2]
    parts = message[rows + 8 :].astype(jnp.float32)
    count = parts.shape[0] // 2
    return (parts[:count] + parts[count:] * 2.0**-11) * jnp.exp2(exponent - 14.0)


def exchanged_small(sent, received, rows):
    return opened_small(sent, rows) + opened_small(received, rows)


def opened(message, rows):
    exponent = message[rows : rows + 8].astype(jnp.float32)[:1]
    (scale,) = tie(jnp.exp2(exponent - 14.0))
    return message[:rows].astype(jnp.float32) * scale, exponent


def added(total, exponent, message):
    rows = total.shape[0]
    received = message[rows : rows + 8].astype(jnp.float32)[:1]
    scale, larger = tie(jnp.exp2(received - 14.0), jnp.maximum(received, exponent) + 1.0)
    return total + message[:rows].astype(jnp.float32) * scale, larger


def half_of(total, axis_name, mask, other=False):
    bit = jnp.minimum(lax.axis_index(axis_name) & mask, 1)
    return part_of(total, 1 - bit if other else bit, 2)


def gather_pair(values, received, axis_name, mask):
    bit = jnp.minimum(lax.axis_index(axis_name) & mask, 1)
    size = values.shape[0]
    whole = jnp.zeros((2 * size,) + values.shape[1:], values.dtype)
    whole = lax.dynamic_update_slice_in_dim(whole, values, bit * size, axis=0)
    return lax.dynamic_update_slice_in_dim(whole, received, (1 - bit) * size, axis=0)


def gelu_share(values):
    return 0.5 * lax.erf(values * 0.5**0.5) + 0.5


def gelu_slope(values):
    return gelu_share(values) + values * jnp.exp(-0.5 * values * values) * 0.3989422804014327


def row_mean(values):
    return jnp.sum(values, axis=-1, keepdims=True) * (1.0 / values.shape[-1])


def placing_kernel(per_owner, owners_in, lengths_in, waveform_in, weight, out, *refs):
    *pieces, owners, lengths, waveform, semaphores = refs
    copies = [
        pltpu.make_async_copy(owners_in, owners, semaphores.at[0]),
        pltpu.make_async_copy(lengths_in, lengths, semaphores.at[1]),
        pltpu.make_async_copy(waveform_in, waveform, semaphores.at[2]),
    ]
    for piece in pieces:
        size = piece.shape[0]
        start = pl.multiple_of(lax.rem(lax.axis_index("dp"), 2) * size, size)
        copies.append(
            pltpu.make_async_copy(weight.at[pl.ds(start, size), :], piece, semaphores.at[3])
        )
    for copy in copies:
        copy.start()
    samples, width = waveform.shape[1], out.shape[2]
    out[...] = jnp.zeros_like(out)
    for copy in copies[:3]:
        copy.wait()
    for row in range(waveform.shape[0]):
        slot = owners[row] * per_owner
        for earlier in range(row if per_owner > 1 else 0):
            slot += jnp.where(owners[earlier] == owners[row], 1, 0)
        out[slot, :, :samples] = waveform[row : row + 1, :]
        length = lengths[row].astype(jnp.float32)
        out[slot, :, width - 128 :] = jnp.full((1, 128), length, jnp.float32)
    for copy in copies[3:]:
        copy.wait()


def placed_rows(owners, lengths, waveform, weight, peers, halved):
    rows, samples = waveform.shape
    per_owner = max(1, 2 * rows // peers)
    width = -(-samples // 128) * 128 + 128
    shapes = [jax.ShapeDtypeStruct((peers * per_owner, 1, width), jnp.float32)]
    if halved:
        shapes.append(jax.ShapeDtypeStruct((weight.shape[0] // 2, weight.shape[1]), weight.dtype))
    arrays = [
        pltpu.with_memory_space_constraint(array, pltpu.HBM)
        for array in (owners, lengths, waveform, weight)
    ]
    return pl.pallas_call(
        functools.partial(placing_kernel, per_owner),
        out_shape=shapes,
        in_specs=[pl.BlockSpec(memory_space=pl.ANY)] * 4,
        out_specs=[pl.BlockSpec(memory_space=pltpu.VMEM)] * len(shapes),
        scratch_shapes=[
            pltpu.SMEM((rows,), jnp.int32),
            pltpu.SMEM((rows,), jnp.int32),
            pltpu.VMEM((rows, samples), jnp.float32),
            pltpu.SemaphoreType.DMA((4,)),
        ],
        compiler_params=pltpu.CompilerParams(vmem_limit_bytes=3 << 20),
    )(*arrays)


def first_raw(windows, weight):
    return jnp.dot(
        windows[...],
        weight[...],
        precision=HIGHEST,
        preferred_element_type=jnp.float32,
    )


def unit_of(raw):
    centered = raw - row_mean(raw)
    scale = lax.rsqrt(row_mean(centered * centered) + epsilon)
    return centered * scale, scale


def blocks_of(total, size):
    return [slice(start, min(start + size, total)) for start in range(0, total, size)]


def folded(values):
    return jnp.sum(values.reshape(-1, 8, values.shape[-1]), axis=0)


def first_kernel(samples, got, weight, vectors, act, owned, raw):
    slots, rows = got.shape[0], owned.shape[0]
    present = jnp.where(got[:, got.shape[1] - 128 :] > 0.5, 1.0, 0.0)
    below = lax.broadcasted_iota(jnp.int32, (slots, slots), 0) >= lax.broadcasted_iota(
        jnp.int32, (slots, slots), 1
    )
    arrival = jnp.dot(
        jnp.where(below, 1.0, 0.0), present, preferred_element_type=jnp.float32
    ).astype(jnp.int32)
    lane = lax.broadcasted_iota(jnp.int32, (slots, 128), 1)
    picking = jnp.where(arrival == lane + 1, present, 0.0)[:, :rows]
    owned[...] = lax.dot_general(
        picking,
        got[...],
        (((0,), (0,)), ((), ())),
        precision=HIGHEST,
        preferred_element_type=jnp.float32,
    )
    frames = raw.shape[0] // rows
    even = (frames + 1) // 2
    lanes = weight.shape[0]
    wave = owned[:, :lanes]
    moved = pltpu.roll(wave, lanes - 5, 1)
    position = lax.broadcasted_iota(jnp.int32, (rows, lanes), 1)
    position = jnp.where(position < samples, lax.div(position, jnp.int32(10)), -1)
    for base, count, values in ((0, even, wave), (even, frames - even, moved)):
        parts = [jnp.where(position == time, values, 0.0) for time in range(count)]
        raw[base * rows : (base + count) * rows, :] = jnp.dot(
            jnp.concatenate(parts, axis=0),
            weight[...],
            precision=HIGHEST,
            preferred_element_type=jnp.float32,
        )
    gains, shifts = vectors[0:1, :], vectors[1:2, :]
    for block in blocks_of(raw.shape[0], 32):
        normed = unit_of(raw[block, :])[0] * gains + shifts
        act[block, :] = (normed * gelu_share(normed)).astype(jnp.bfloat16)


def first_layer(rows, samples, got, weight, vectors):
    shape = ((samples // 5 - 1) * rows, weight.shape[1])
    return pl.pallas_call(
        functools.partial(first_kernel, samples),
        out_shape=[
            jax.ShapeDtypeStruct(shape, jnp.bfloat16),
            jax.ShapeDtypeStruct((rows, got.shape[1]), jnp.float32),
        ],
        scratch_shapes=[pltpu.VMEM(shape, jnp.float32)],
        compiler_params=pltpu.CompilerParams(vmem_limit_bytes=8 << 20),
    )(got, weight, vectors)


def back_kernel(
    windows, windows_across, first_weight, vectors, weight, padded, sums, small, raw, grad
):
    later_rows = raw.shape[0] - padded.shape[0]
    even_rows, channels = padded.shape
    step = even_rows - later_rows
    raw[...] = first_raw(windows, first_weight)

    def pulled(values, tap):
        return lax.dot_general(
            values,
            weight[tap * channels : (tap + 1) * channels, :],
            (((1,), (1,)), ((), ())),
            preferred_element_type=jnp.float32,
        )

    values = padded[...]
    latest = pulled(values, 2)
    grad[:even_rows, :] = pulled(values, 0)
    grad[step:even_rows, :] += latest[:later_rows]
    grad[even_rows:, :] = pulled(values, 1)[:later_rows]
    gains, shifts = vectors[0:1, :], vectors[1:2, :]
    gain_sum = jnp.zeros((8, channels), jnp.float32)
    shift_sum = jnp.zeros((8, channels), jnp.float32)
    for rows in blocks_of(raw.shape[0], 40):
        unit, scale = unit_of(raw[rows, :])
        grad_out = grad[rows, :] * gelu_slope(unit * gains + shifts)
        grad_unit = grad_out * gains
        grad[rows, :] = scale * (
            grad_unit - row_mean(grad_unit) - unit * row_mean(grad_unit * unit)
        )
        gain_sum += folded(grad_out * unit)
        shift_sum += folded(grad_out)
    taps = windows_across.shape[0]
    small[:taps, :] = jnp.dot(
        windows_across[...], grad[...], precision=HIGHEST, preferred_element_type=jnp.float32
    )
    small[taps : taps + 1, :] = jnp.sum(gain_sum, axis=0, keepdims=True)
    small[taps + 1 : taps + 2, :] = jnp.sum(shift_sum, axis=0, keepdims=True)
    small[taps + 2 :, :] = sums[:4, :]


def backward(windows, windows_across, first_weight, vectors, weight, padded, sums):
    frames, channels = windows.shape[0], vectors.shape[1]
    return pl.pallas_call(
        back_kernel,
        out_shape=jax.ShapeDtypeStruct((windows.shape[1] + 6, channels), jnp.float32),
        scratch_shapes=[pltpu.VMEM((frames, channels), jnp.float32)] * 2,
        compiler_params=pltpu.CompilerParams(vmem_limit_bytes=8 << 20),
    )(windows, windows_across, first_weight, vectors, weight, padded, sums)


def head_kernel(groups, place, act, *refs):
    *weights, target, valid, vectors = refs[:-8]
    weight_out, padded, logvar, sums, message, weight, grad, semaphore = refs[-8:]
    later_rows, channels = target.shape[0], vectors.shape[1]
    even_rows = padded.shape[0]
    step = even_rows - later_rows
    depth = weight.shape[0]
    half = depth // groups // 2
    group, core = place[0], place[1]
    if len(weights) == 1:
        places = [slice(None)]
    else:
        base = (1 - group) * 2 * half
        places = [
            pl.ds(pl.multiple_of(group * 2 * half, half), 2 * half),
            pl.ds(pl.multiple_of(base + core * half, half), half),
            pl.ds(pl.multiple_of(base + (1 - core) * half, half), half),
        ]
    copies = [
        pltpu.make_async_copy(source, weight.at[rows, :], semaphore.at[index])
        for index, (source, rows) in enumerate(zip(weights, places))
    ]
    for copy in copies:
        copy.start()
    for copy in copies:
        copy.wait()
    copy = pltpu.make_async_copy(weight, weight_out, semaphore.at[3])
    copy.start()

    def matmul(left, right):
        return jnp.dot(left, right, preferred_element_type=jnp.float32)

    even, odd = act[:even_rows, :], act[even_rows:, :]
    latest = matmul(even, weight[2 * channels :, :])
    grad[:later_rows, :] = (
        matmul(even, weight[:channels, :])[:later_rows]
        + matmul(odd, weight[channels : 2 * channels, :])
        + latest[step:]
    )
    gains, shifts = vectors[2:3, :], vectors[3:4, :]
    block = 3 * step if later_rows % (3 * step) == 0 else step
    last = jnp.concatenate([valid[...]] * (block // step), axis=0)
    times = lax.broadcasted_iota(jnp.int32, (block, 1), 0)
    gain_sum = jnp.zeros((8, channels), jnp.float32)
    shift_sum = jnp.zeros((8, channels), jnp.float32)
    largest = jnp.zeros((8, channels), jnp.float32)
    loss_sum = jnp.zeros((block, 1), jnp.float32)
    count = jnp.zeros((block, 1), jnp.float32)
    for rows in blocks_of(later_rows, block):
        unit, scale = unit_of(grad[rows, :])
        normed = unit * gains + shifts
        share = gelu_share(normed)
        slope = share + normed * (jnp.exp(-0.5 * normed * normed) * 0.3989422804014327)
        active = normed * share
        active = active - row_mean(active)
        variance = row_mean(active * active) + epsilon
        raw_logvar = jnp.log(variance)
        frame_mask = jnp.where(times + rows.start < last, 1.0, 0.0)
        logvar[rows, :] = raw_logvar * frame_mask
        misfit = raw_logvar - target[rows, :]
        weighted = frame_mask * misfit
        loss_sum += weighted * misfit
        count += frame_mask
        grad_out = weighted / variance * (4.0 / channels) * active * slope
        grad_unit = grad_out * gains
        result = scale * (grad_unit - row_mean(grad_unit) - unit * row_mean(grad_unit * unit))
        gain_sum += folded(grad_out * unit)
        shift_sum += folded(grad_out)
        largest = jnp.maximum(
            largest, jnp.max(jnp.abs(result).reshape(-1, 8, channels), axis=0)
        )
        grad[rows, :] = result
    sums[0:1, :] = jnp.sum(gain_sum, axis=0, keepdims=True)
    sums[1:2, :] = jnp.sum(shift_sum, axis=0, keepdims=True)
    sums[2:3, :] = jnp.broadcast_to(jnp.sum(loss_sum, axis=0, keepdims=True), (1, channels))
    sums[3:4, :] = jnp.broadcast_to(jnp.sum(count, axis=0, keepdims=True), (1, channels))
    sums[4:8, :] = jnp.zeros((4, channels), jnp.float32)
    patch_bound = channels**0.5 * jnp.max(
        jnp.abs(vectors[0:1, :]), axis=1, keepdims=True
    ) + jnp.max(jnp.abs(vectors[1:2, :]), axis=1, keepdims=True)
    grad[later_rows:, :] = jnp.zeros((step, channels), jnp.float32)
    padded[...] = grad[...].astype(jnp.bfloat16)
    bound = jnp.max(largest, axis=0, keepdims=True) * 1.01 * (later_rows * patch_bound)
    exponent = jnp.ceil(jnp.log2(jnp.maximum(bound, 1e-30)))
    sums[8:, :] = jnp.broadcast_to(exponent, (8, channels))
    middle = channels // 2
    away = pl.ds(pl.multiple_of((1 - core) * middle, middle), middle)
    message[:even_rows, :] = grad[:, away].astype(jnp.bfloat16)
    message[even_rows:, :] = sums[8:, away].astype(jnp.bfloat16)
    copy.wait()


def head(groups, place, act, weights, target, valid, vectors):
    channels = act.shape[1]
    depth = 3 * channels
    later_rows = target.shape[0]
    even_rows = act.shape[0] - later_rows
    shapes = [
        pltpu.HBM((depth, channels), jnp.bfloat16),
        pltpu.VMEM((even_rows, channels), jnp.bfloat16),
        pltpu.HBM((later_rows, 1), jnp.float32),
        pltpu.VMEM((16, channels), jnp.float32),
        pltpu.VMEM((even_rows + 8, channels // 2), jnp.bfloat16),
    ]
    weights = [pltpu.with_memory_space_constraint(part, pltpu.HBM) for part in weights[:2]] + weights[2:]
    arrays = [act, *weights, target, valid, vectors]
    return pl.pallas_call(
        functools.partial(head_kernel, groups),
        out_shape=shapes,
        in_specs=[
            pl.BlockSpec(memory_space=pltpu.SMEM),
            pl.BlockSpec(memory_space=pltpu.VMEM),
        ]
        + [pl.BlockSpec(memory_space=pl.ANY)] * len(weights)
        + [pl.BlockSpec(memory_space=pltpu.VMEM)] * 3,
        out_specs=[pl.BlockSpec(memory_space=pltpu.HBM)]
        + [pl.BlockSpec(memory_space=pltpu.VMEM)] * (len(shapes) - 1),
        scratch_shapes=[
            pltpu.VMEM((depth, channels), jnp.bfloat16),
            pltpu.VMEM((even_rows, channels), jnp.float32),
            pltpu.SemaphoreType.DMA((4,)),
        ],
        compiler_params=pltpu.CompilerParams(vmem_limit_bytes=8 << 20),
    )(place, *arrays)


def split_kernel(
    groups,
    place,
    own_act,
    other_act,
    own_grad,
    received,
    own_note,
    near_message,
    near_kept,
    far_message,
    far_kept,
    note,
    product,
):
    depth, middle = product.shape
    even_rows = own_grad.shape[0]
    later_rows = own_act.shape[0] - even_rows
    step, channels = even_rows - later_rows, own_act.shape[1]
    quarter = middle // 2
    core, bit, side = place[0], place[1], place[2]
    columns = pl.ds(pl.multiple_of(core * middle, middle), middle)

    def outer(left, right):
        return lax.dot_general(
            left, right, (((0,), (0,)), ((), ())), preferred_element_type=jnp.float32
        )

    def shifted(values):
        values = values[:later_rows].astype(jnp.float32)
        zeros = jnp.zeros((step, middle), jnp.float32)
        return jnp.concatenate([zeros, values], axis=0).astype(jnp.bfloat16)

    own, other = own_grad[:, columns], received[:even_rows, :]
    own_even, own_odd = own_act[:even_rows, :], own_act[even_rows:, :]
    other_even, other_odd = other_act[:even_rows, :], other_act[even_rows:, :]
    product[:channels, :] = outer(own_even, own) + outer(other_even, other)
    product[channels : 2 * channels, :] = outer(own_odd, own[:later_rows]) + outer(
        other_odd, other[:later_rows]
    )
    product[2 * channels :, :] = outer(own_even, shifted(own)) + outer(other_even, shifted(other))

    larger = jnp.maximum(own_note[8:, columns], received[even_rows:, :].astype(jnp.float32)) + 1.0
    note[...] = larger
    near, far = slice(0, quarter), slice(quarter, middle)
    stay, size = depth // 2, depth // groups
    cut = size // 2
    near_message[:stay, :] = product[
        pl.ds(pl.multiple_of((1 - bit) * stay, 16), stay), near
    ].astype(jnp.bfloat16)
    near_message[stay:, :] = larger[:, near].astype(jnp.bfloat16)
    far_message[stay:, :] = larger[:, far].astype(jnp.bfloat16)
    for index in range(groups):
        rows = slice(index * cut, (index + 1) * cut)
        away = pl.ds(pl.multiple_of(index * size + (1 - side) * cut, 16), cut)
        far_message[rows, :] = product[away, far].astype(jnp.bfloat16)
        far_kept[rows, :] = product[pl.ds(pl.multiple_of(index * size + side * cut, 16), cut), far]
    near_kept[...] = product[pl.ds(pl.multiple_of(bit * stay, 16), stay), near]


def split(groups, place, own_act, other_act, own_grad, received, note):
    channels = own_act.shape[1]
    depth, quarter = 3 * channels, channels // 4
    message = jax.ShapeDtypeStruct((depth // 2 + 8, quarter), jnp.bfloat16)
    part = jax.ShapeDtypeStruct((depth // 2, quarter), jnp.float32)
    shapes = [message, part, message, part, jax.ShapeDtypeStruct((8, 2 * quarter), jnp.float32)]
    return pl.pallas_call(
        functools.partial(split_kernel, groups),
        out_shape=shapes,
        in_specs=[pl.BlockSpec(memory_space=pltpu.SMEM)]
        + [pl.BlockSpec(memory_space=pltpu.VMEM)] * 5,
        out_specs=[pl.BlockSpec(memory_space=pltpu.VMEM)] * len(shapes),
        scratch_shapes=[pltpu.VMEM((depth, 2 * quarter), jnp.float32)],
        compiler_params=pltpu.CompilerParams(vmem_limit_bytes=8 << 20),
    )(place, own_act, other_act, own_grad, received, note)


def storing_kernel(last, flips, *refs):
    own, other, out, semaphores = refs[-4:]
    if len(refs) > 5:
        own, other, small, out, weight_out, *vectors_out, loss_out, semaphores = refs
    me = lax.axis_index("dp")
    core, side, bit = lax.rem(me, 2), lax.rem(me // 2, 2), lax.rem(me // last, 2)
    size, middle = out.shape[0] // 4, own.shape[1]
    copies = []
    for index, (side_flip, bit_flip) in enumerate(flips):
        block = (side + side_flip - 2 * side * side_flip) * 2 + (bit + bit_flip - 2 * bit * bit_flip)
        rows = pl.ds(pl.multiple_of(block * size, 8), size)
        for number, (source, column) in enumerate(((own, core), (other, 1 - core))):
            columns = pl.ds(pl.multiple_of(column * middle, middle), middle)
            copies.append(
                pltpu.make_async_copy(
                    source.at[index * size : (index + 1) * size, :],
                    out.at[rows, columns],
                    semaphores.at[2 * index + number],
                )
            )
    for copy in copies:
        copy.start()
    if len(refs) > 5:
        count, quarter = small.shape[0] // 2, small.shape[1] // 2
        rows = jnp.concatenate(
            [
                small[start : start + count, place : place + quarter]
                for place in (0, quarter)
                for start in (0, count)
            ],
            axis=1,
        )
        taps = weight_out.shape[0]
        weight_out[...] = rows[:taps]
        for index, vector_out in enumerate(vectors_out):
            vector_out[...] = rows[taps + index : taps + index + 1]
        loss_out[...] = rows[taps + 4 : taps + 5] / rows[taps + 5 :]
    for copy in copies:
        copy.wait()


def stored(last, flips, shape, before, own, other, small=None):
    blocks = [own, other] if small is None else [own, other, small]
    shapes = [pltpu.HBM(shape, jnp.float32)]
    if small is not None:
        taps = small.shape[0] // 2 - 6
        shapes.append(jax.ShapeDtypeStruct((taps, shape[1]), jnp.float32))
        shapes += [jax.ShapeDtypeStruct((1, shape[1]), jnp.float32)] * 5
    return pl.pallas_call(
        functools.partial(storing_kernel, last, flips),
        out_shape=shapes,
        in_specs=[pl.BlockSpec(memory_space=pl.ANY)] * len(before)
        + [pl.BlockSpec(memory_space=pltpu.VMEM)] * len(blocks),
        out_specs=[pl.BlockSpec(memory_space=pl.ANY)]
        + [pl.BlockSpec(memory_space=pltpu.VMEM)] * (len(shapes) - 1),
        scratch_shapes=[pltpu.SemaphoreType.DMA((2 * len(flips),))],
        input_output_aliases={0: 0} if before else {},
        compiler_params=pltpu.CompilerParams(vmem_limit_bytes=3 << 20),
    )(*before, *blocks)


def added_plain(total, exponent, message):
    rows = total.shape[0]
    received = message[rows : rows + 8].astype(jnp.float32)[:1]
    (larger,) = tie(jnp.maximum(received, exponent) + 1.0)
    return total + message[:rows].astype(jnp.float32), larger


def per_device(
    waveform,
    lengths,
    owner_of,
    targets,
    first_weight,
    first_gain,
    first_shift,
    second_weight,
    second_gain,
    second_shift,
):
    peers, groups = lax.axis_size("dp"), lax.axis_size("fsdp")
    rows, samples = waveform.shape
    later = targets.shape[1]
    frames = samples // 5 - 1
    channels = first_weight.shape[1]
    staged = power_of_two(peers) and power_of_two(groups) and peers >= 16 and groups > 1
    core, side = lax.axis_index("dp") % 2, lax.axis_index("dp") // 2 % 2

    vectors = jnp.stack([first_gain, first_shift, second_gain, second_shift] * 2)

    fetched = None
    if staged and groups == 2:
        sent, fetched = placed_rows(owner_of, lengths, waveform, second_weight, peers, True)
        fetched = swap(fetched, "fsdp", 1)
    else:
        (sent,) = placed_rows(owner_of, lengths, waveform, second_weight, peers, False)
    got = lax.all_to_all(sent, "dp", split_axis=0, concat_axis=0, tiled=True)
    got = got.reshape(sent.shape[0], sent.shape[2])
    if fetched is not None:
        got, fetched, vectors = tie(got, fetched, vectors)
        fetched_others = swap(fetched, "dp", 1)
    lanes = got.shape[1] - 128
    repeats = -(-lanes // first_weight.shape[0])
    repeated = jnp.tile(first_weight, (repeats, 1))[:lanes]
    act, owned = first_layer(rows, samples, got, repeated, vectors)
    waveform, lengths = owned[:, :samples], owned[:, -1].astype(jnp.int32)

    blocks = waveform.reshape(rows, later + 1, 2, 5).transpose(1, 2, 0, 3)
    earlier_block, later_block = blocks[:, 0], blocks[:, 1]
    windows = jnp.concatenate(
        [
            jnp.concatenate([earlier_block, later_block], axis=2),
            jnp.concatenate([later_block[:later], earlier_block[1:]], axis=2),
        ],
        axis=0,
    ).reshape(frames * rows, 10)
    if fetched is None:
        weights = [lax.all_gather(second_weight, "fsdp", axis=0, tiled=True)]
    else:
        weights = [second_weight, fetched, fetched_others]
    first = (first_weight, vectors)
    windows_across = windows.T
    if staged:
        act_other = swap(act, "dp", 1)

    first_valid = (lengths - 10) // 5 + 1
    second_valid = ((first_valid - 3) // 2 + 1) * rows
    weight, padded, flat_logvar, sums, message = head(
        groups,
        jnp.stack([lax.axis_index("fsdp"), core]),
        act,
        weights,
        targets.T.reshape(later * rows, 1),
        second_valid[:, None],
        vectors,
    )

    if staged:
        group_rows = 3 * channels // groups
        middle, quarter = channels // 2, channels // 4
        strides = [1 << bit for bit in range(2, peers.bit_length() - 1)]
        group_strides = [1 << bit for bit in range(groups.bit_length() - 2, -1, -1)]
        top = group_strides[0]
        received = swap(message, "dp", 1)
        bit = jnp.minimum(lax.axis_index("fsdp") & top, 1)
        near_message, near, far_message, far, note = split(
            groups, jnp.stack([core, bit, side]), act, act_other, padded, received, sums
        )
        near_exponent, far_exponent = note[:1, :quarter], note[:1, quarter:]
        padded, near_message, far_message = tie(padded, near_message, far_message)
        small = backward(windows, windows_across, *first, weight, padded, sums)
        far, far_exponent = added_plain(far, far_exponent, swap(far_message, "dp", 2))
        received = swap(near_message, "fsdp", top)
        near, near_exponent = added_plain(near, near_exponent, received)
        for mask in group_strides[1:]:
            near_message = packed(half_of(near, "fsdp", mask, True), near_exponent)
            received = swap(near_message, "fsdp", mask)
            near, near_exponent = added(half_of(near, "fsdp", mask), near_exponent, received)
        near_message = packed(half_of(near, "dp", 2, True), near_exponent)
        small = jnp.concatenate(
            [small[:, start : start + quarter] for start in range(0, channels, quarter)], axis=0
        )
        for mask in group_strides:
            sent = half_of(far, "fsdp", mask, True)
            far_message = packed(sent, far_exponent, small)
            near_message, far_message = tie(near_message, far_message)
            received = swap(far_message, "fsdp", mask)
            small = exchanged_small(far_message, received, sent.shape[0])
            far, far_exponent = added(half_of(far, "fsdp", mask), far_exponent, received)
        received = swap(near_message, "dp", 2)
        near, near_exponent = added(half_of(near, "dp", 2), near_exponent, received)
        total = jnp.concatenate([near, far], axis=1)
        exponent = jnp.concatenate([near_exponent, far_exponent], axis=1)
        count = small.shape[0] // 2
        small = jnp.concatenate([small[:count], small[count:]], axis=1)

        for mask in strides[:-1]:
            sent = half_of(total, "dp", mask, True)
            message = packed(sent, exponent, small)
            received = swap(message, "dp", mask)
            small = exchanged_small(message, received, sent.shape[0])
            total, exponent = added(half_of(total, "dp", mask), exponent, received)
        piece = total.shape[0]
        for mask in strides[-1:]:
            message = packed(total, exponent, small)
            received = swap(message, "dp", mask)
            small = exchanged_small(message, received, piece)
            total, exponent = opened(message, piece)
            total, exponent = added(total, exponent, received)
        message = packed(total, exponent)
        for mask in strides[-2:0:-1]:
            message = gather_pair(message, swap(message, "dp", mask), "dp", mask)

        last = strides[0]
        rows_sent = message.shape[0]

        def extended(message, small):
            extra, exponent = scaled_rows(small)
            exponent = jnp.broadcast_to(exponent, (8, middle))
            extra = jnp.concatenate([exponent, extra], axis=0).astype(jnp.float16)
            return jnp.concatenate([message, extra], axis=0)

        sent = extended(message, small)
        received = swap(sent, "dp", 2)
        beside = swap(message, "dp", last)
        small = exchanged_small(sent, received, rows_sent)
        across = received[:rows_sent]
        cut = rows_sent // 16 * 8
        upper = swap(beside[:cut], "dp", 2)
        lower = swap(across[cut:], "dp", last)
        early = jnp.concatenate([message, beside, across], axis=0)
        sent = extended(early, small)
        received = swap(sent, "dp", 1)
        small = exchanged_small(sent, received, early.shape[0])
        early_other = received[: early.shape[0]]
        corner = jnp.concatenate([upper, lower], axis=0)

        def opened_blocks(blocks):
            blocks = blocks.reshape(-1, piece + 8, middle)
            (scale,) = tie(jnp.exp2(blocks[:, piece:, :].astype(jnp.float32)[:, :1] - 14.0))
            return (blocks[:, :piece].astype(jnp.float32) * scale).reshape(-1, middle)

        shape = (group_rows, channels)
        flips = ((0, 0), (0, 1), (1, 0))
        gradient, *sums_out = stored(
            last, flips, shape, (), opened_blocks(early), opened_blocks(early_other), small
        )
        corner, gradient = tie(corner, gradient)
        corner_other = swap(corner, "dp", 1)
        (grad_weight_two,) = stored(
            last, ((1, 1),), shape, (gradient,), opened_blocks(corner), opened_blocks(corner_other)
        )
    else:
        even, odd = act[: padded.shape[0]], act[padded.shape[0] :]
        zeros = jnp.zeros((rows, channels), padded.dtype)
        shifted = jnp.concatenate([zeros, padded[: later * rows]], axis=0)
        pairs = [(even, padded), (odd, padded[: later * rows]), (even, shifted)]
        partial = [
            lax.dot_general(
                left, right, (((0,), (0,)), ((), ())), preferred_element_type=jnp.float32
            )
            for left, right in pairs
        ]
        partial = jnp.concatenate(partial, axis=0)
        partial = lax.psum_scatter(partial, "fsdp", scatter_dimension=0, tiled=True)
        grad_weight_two = lax.psum(partial, "dp")
        small = backward(windows, windows_across, *first, weight, padded, sums)
        small = lax.psum(small, ("dp", "fsdp"))
        sums_out = [small[:10], *(small[row : row + 1] for row in range(10, 14))]
        sums_out.append(small[14:15] / small[15:16])

    logvar = flat_logvar.reshape(later, rows).T
    grad_weight_one, *vectors_out, loss = sums_out
    vectors_out = [vector.reshape(channels) for vector in vectors_out]
    return (logvar, loss[0, 0], grad_weight_two, grad_weight_one, *vectors_out)


def solution(mesh):
    placed = (
        P(("dp", "fsdp"), None),
        P(("dp", "fsdp")),
        P(("dp", "fsdp")),
        P(("dp", "fsdp"), None),
        P(),
        P(),
        P(),
        P("fsdp", None),
        P(),
        P(),
    )

    return jax.shard_map(
        per_device,
        mesh=mesh,
        in_specs=placed,
        out_specs=(P(("dp", "fsdp"), None), P(), P("fsdp", None), P(), P(), P(), P(), P()),
        check_vma=False,
    )
```
